32 devices in a mesh: batch: 4 (over y, x), seq: 8 (over z, core).
Axes of the slice: x: 2, y: 2, z: 4, core: 2. Of those that a mesh axis runs over, the one named last changes fastest.
Arguments:
- block_input: bfloat16 [4, 1024, 2048], P('batch', 'seq'), may hold values from -6 to 6
- cotangent: bfloat16 [4, 1024, 2048], P('batch', 'seq'), may hold values from -6 to 6
- init_state: float32 [4, 16, 4096], P('batch'), may hold values from -3 to 3
- doc_starts: int32 [4, 3], P('batch'), may hold values from 8 to 1016, as said below
- norm_gain: bfloat16 [2048], P(('batch', 'seq')), may hold values from 0.5 to 1.5
- in_weight: bfloat16 [2048, 8192], P(('batch', 'seq')), may hold values from -0.125 to 0.125
- conv_weight: bfloat16 [4, 4096], P(None, ('batch', 'seq')), may hold values from -3 to 3
- conv_bias: bfloat16 [4096], P(('batch', 'seq')), may hold values from -0.5 to 0.5
- xproj_weight: bfloat16 [4096, 160], P(('batch', 'seq')), may hold values from -0.09375 to 0.09375
- dtproj_weight: bfloat16 [128, 4096], P(None, ('batch', 'seq')), may hold values from -0.5 to 0.5
- dt_bias: bfloat16 [4096], P(('batch', 'seq')), may hold values from -6.875 to -2.296875
- decay_log: bfloat16 [16, 4096], P(None, ('batch', 'seq')), may hold values from 0 to 2.765625
- skip_gain: bfloat16 [4096], P(('batch', 'seq')), may hold values from 0.5 to 1.5
- out_weight: bfloat16 [4096, 2048], P(('batch', 'seq')), may hold values from -0.25 to 0.25
Outputs:
- block_output: bfloat16 [4, 1024, 2048], P('batch', 'seq')
- input_grad: bfloat16 [4, 1024, 2048], P('batch', 'seq')
- final_state: float32 [4, 16, 4096], P('batch', None, 'seq')
- init_grad: float32 [4, 16, 4096], P('batch', None, 'seq')
- gain_grad: float32 [2048], P(('batch', 'seq'))
- in_weight_grad: float32 [2048, 8192], P(('batch', 'seq'))
- conv_weight_grad: float32 [4, 4096], P(None, ('batch', 'seq'))
- conv_bias_grad: float32 [4096], P(('batch', 'seq'))
- xproj_grad: float32 [4096, 160], P(('batch', 'seq'))
- dtproj_grad: float32 [128, 4096], P(None, ('batch', 'seq'))
- dt_bias_grad: float32 [4096], P(('batch', 'seq'))
- decay_log_grad: float32 [16, 4096], P(None, ('batch', 'seq'))
- skip_grad: float32 [4096], P(('batch', 'seq'))
- out_weight_grad: float32 [4096, 2048], P(('batch', 'seq'))
The draws below stay inside these ranges and needn't reach their ends.
Inputs may be any that keep to these rules, and one draw needn't show every extreme that they name: `doc_starts`: each row holds 3 strictly increasing positions, each a positive multiple of 8 below 1024: the first positions of the row's second and later documents.
All inputs are finite; a program needn't handle non-finite values.
Results may differ from the reference program's by a relative error of at most 0.012.
Values may be sent and summed in bfloat16 or wider, within the bound.
A program may use at most 256 MiB of HBM per device.

```python
import jax
import jax.numpy as jnp
from jax import lax

D_MODEL = 2048
D_INNER = 4096
D_STATE = 16
DT_RANK = 128
KCONV = 4
GRAIN = 8
CUTS = 3
LENGTH = 1024
ROWS = 4


def draw_doc_starts(key, part):
    blocks = LENGTH // GRAIN

    def row_cuts(row_key, forced):
        shuffled = jax.random.permutation(row_key, blocks - 1) + 1
        picked = jnp.sort(shuffled[:CUTS])
        inner = jax.random.permutation(jax.random.fold_in(row_key, 5), blocks - 3) + 2
        ends = jnp.concatenate([jnp.ones((1,), jnp.int32), jnp.sort(inner[:CUTS - 2]).astype(jnp.int32), jnp.full((1,), blocks - 1, jnp.int32)])
        return jnp.where(forced, ends, picked.astype(jnp.int32)) * GRAIN
    row_keys = jax.random.split(jax.random.fold_in(key, 11), ROWS)
    forced_rows = jnp.arange(ROWS, dtype=jnp.int32) == 0
    return jax.vmap(row_cuts)(row_keys, forced_rows).astype(jnp.int32)


def block_scale(rng, shape, cuts, low, largest):
    def one(dim, parts):
        draws = jax.random.uniform(jax.random.fold_in(jax.random.fold_in(rng, 6), dim), (parts,), jnp.float32, low / len(cuts), largest / len(cuts))
        return jnp.repeat(jnp.exp(draws), shape[dim] // parts).reshape((-1,) + (1,) * (len(shape) - dim - 1))

    loudness = one(*cuts[0])
    for cut in cuts[1:]:
        loudness = loudness * one(*cut)
    return loudness


def gaussian(rng, shape, spread, limit, pieces=(), held_as=jnp.bfloat16):
    drawn = jax.random.normal(rng, shape, jnp.float32) * spread
    if len(pieces) > 0:
        drawn = block_scale(rng, shape, pieces, -0.22, 0.18) * drawn
    return jnp.clip(drawn, min=-limit, max=limit).astype(held_as)


def setup_inputs(seed: int = 0) -> dict:
    splits = jax.random.split(jax.random.key(seed), 15)
    block_input = gaussian(splits[0], (ROWS, LENGTH, D_MODEL), 1.0, 6.0, ((0, 4), (1, 8)))
    cotangent = gaussian(splits[1], (ROWS, LENGTH, D_MODEL), 1.0, 6.0, ((0, 4), (1, 8)))
    init_state = gaussian(splits[2], (ROWS, D_STATE, D_INNER), 0.5, 3.0, ((0, 4),), jnp.float32)
    doc_starts = draw_doc_starts(jax.random.fold_in(splits[14], 71), 0)
    norm_gain = jnp.clip(1.0 + 0.1 * jax.random.normal(splits[4], (D_MODEL,), jnp.float32), 0.5, 1.5).astype(jnp.bfloat16)
    in_weight = gaussian(splits[5], (D_MODEL, 2 * D_INNER), D_MODEL ** -0.5, 0.125, ((0, 32),))
    conv_weight = gaussian(splits[6], (KCONV, D_INNER), KCONV ** -0.5, 3.0, ((1, 32),))
    conv_bias = jnp.clip(jax.random.uniform(splits[7], (D_INNER,), jnp.float32, -0.5, 0.5) * block_scale(splits[7], (D_INNER,), ((0, 32),), -0.4, 0.0), -0.5, 0.5).astype(jnp.bfloat16)
    xproj_weight = gaussian(splits[8], (D_INNER, DT_RANK + 2 * D_STATE), D_INNER ** -0.5, 0.09375, ((0, 32),))
    dtproj_weight = gaussian(splits[9], (DT_RANK, D_INNER), DT_RANK ** -0.5, 0.5, ((1, 32),))
    dt_bias = jnp.clip(-6.875 + 4.578125 * jax.random.uniform(splits[10], (D_INNER,), jnp.float32) ** block_scale(splits[10], (D_INNER,), ((0, 32),), -0.2, 0.2), -6.875, -2.296875).astype(jnp.bfloat16)
    decay_log = jnp.clip(2.765625 * jax.random.uniform(splits[11], (D_STATE, D_INNER), jnp.float32) ** block_scale(splits[11], (D_STATE, D_INNER), ((1, 32),), -0.2, 0.2), 0.0, 2.765625).astype(jnp.bfloat16)
    skip_gain = jnp.clip(0.5 + 1.0 * jax.random.uniform(splits[12], (D_INNER,), jnp.float32) ** block_scale(splits[12], (D_INNER,), ((0, 32),), -0.2, 0.2), 0.5, 1.5).astype(jnp.bfloat16)
    out_weight = gaussian(splits[13], (D_INNER, D_MODEL), (D_INNER // 8) ** -0.5, 0.25, ((0, 32),))
    return dict(block_input=block_input, cotangent=cotangent, init_state=init_state, doc_starts=doc_starts, norm_gain=norm_gain, in_weight=in_weight, conv_weight=conv_weight, conv_bias=conv_bias, xproj_weight=xproj_weight, dtproj_weight=dtproj_weight, dt_bias=dt_bias, decay_log=decay_log, skip_gain=skip_gain, out_weight=out_weight)


EPS = 1e-05
HIGHEST = lax.Precision.HIGHEST

@jax.custom_vjp
def low(v):
    return lax.optimization_barrier(v.astype(jnp.bfloat16)).astype(jnp.float32)

@jax.custom_vjp
def low_back(v):
    return v

def low_keep(v):
    return (low(v), None)

def low_pass(kept, grad):
    return (grad,)

def back_keep(v):
    return (v, None)

def back_low(kept, grad):
    return (low(grad),)
low.defvjp(low_keep, low_pass)
low_back.defvjp(back_keep, back_low)

def matmul(left, right):
    return jnp.dot(left, right, precision=HIGHEST)

def scan_row(step_size, act_in, entry_coef, exit_coef, keep_flag, decay_rate, state_in):
    length = step_size.shape[0]

    def token_step(carried, token_in):
        step_now, act_now, entry_now, exit_now, keep_now = token_in
        carried = jnp.exp(step_now[None, :] * decay_rate) * keep_now * carried + entry_now[:, None] * (step_now * act_now)[None, :]
        return (carried, lax.optimization_barrier(jnp.sum(exit_now[:, None] * carried, axis=0)))

    @jax.checkpoint
    def block_step(carried, inputs):
        return lax.scan(token_step, carried, inputs)
    shaped = tuple((source.reshape((length // GRAIN, GRAIN) + source.shape[1:]) for source in (step_size, act_in, entry_coef, exit_coef, keep_flag)))
    carried, readout = lax.scan(block_step, state_in, shaped)
    return (readout.reshape(length, step_size.shape[1]), carried)

def forward(params, row_x, row_state, row_starts):
    norm_gain, in_weight, conv_weight, conv_bias, xproj_weight, dtproj_weight, dt_bias, decay_log, skip_gain, out_weight = params
    length = row_x.shape[0]
    inner_width = in_weight.shape[1] // 2
    rank_width = dtproj_weight.shape[0]
    state_width = decay_log.shape[0]
    tap_count = conv_weight.shape[0]
    places = jnp.arange(length, dtype=jnp.int32)
    doc_here = lax.optimization_barrier(jnp.sum((places[:, None] >= row_starts[None, :]).astype(jnp.int32), axis=1))
    keep_flag = 1.0 - jnp.any(places[:, None] == row_starts[None, :], axis=1).astype(jnp.float32)
    inv_rms = lax.rsqrt(lax.optimization_barrier(jnp.mean(row_x * row_x, axis=-1, keepdims=True)) + EPS)
    normed = low(row_x * inv_rms * norm_gain)
    mixed_in = low_back(matmul(normed, in_weight))
    conv_in = low(mixed_in[:, :inner_width])
    gate_pre = mixed_in[:, inner_width:]
    padded = jnp.concatenate([jnp.zeros((tap_count - 1, inner_width), jnp.float32), conv_in], axis=0)
    conv_out = jnp.zeros((length, inner_width), jnp.float32) + conv_bias
    for tap_index in range(tap_count):
        back_by = tap_count - 1 - tap_index
        earlier_doc = jnp.concatenate([jnp.zeros((back_by,), jnp.int32), doc_here[:length - back_by]])
        same_doc = (earlier_doc == doc_here).astype(jnp.float32)[:, None]
        conv_out = conv_out + conv_weight[tap_index] * padded[tap_index:tap_index + length] * same_doc
    act_in = low(jax.nn.silu(conv_out))
    projected = low_back(matmul(act_in, xproj_weight))
    rank_in = low(projected[:, :rank_width])
    entry_coef = projected[:, rank_width:rank_width + state_width]
    exit_coef = projected[:, rank_width + state_width:]
    step_linear = low_back(matmul(rank_in, dtproj_weight))
    step_size = jax.nn.softplus(step_linear + dt_bias)
    decay_rate = -jnp.exp(decay_log)
    readout, last_state = scan_row(step_size, act_in, entry_coef, exit_coef, keep_flag, decay_rate, row_state)
    mixed_out = readout + skip_gain * act_in
    gated_out = low(mixed_out * jax.nn.silu(gate_pre))
    return (row_x + matmul(gated_out, out_weight), last_state)

def reference(block_input, cotangent, init_state, doc_starts, norm_gain, in_weight, conv_weight, conv_bias, xproj_weight, dtproj_weight, dt_bias, decay_log, skip_gain, out_weight):
    params = tuple((weight.astype(jnp.float32) for weight in (norm_gain, in_weight, conv_weight, conv_bias, xproj_weight, dtproj_weight, dt_bias, decay_log, skip_gain, out_weight)))

    def row_step(totals, row_inputs):
        row_x, row_cot, row_state, row_starts = row_inputs

        def row_forward(param_set, input_x, input_state):
            return forward(param_set, input_x, input_state, row_starts)
        (row_out, last_state), pull_back = jax.vjp(row_forward, params, row_x.astype(jnp.float32), row_state)
        grad_params, grad_x, grad_state = pull_back((row_cot.astype(jnp.float32), jnp.zeros_like(last_state)))
        totals = jax.tree.map(jnp.add, totals, grad_params)
        return (totals, (row_out.astype(jnp.bfloat16), grad_x.astype(jnp.bfloat16), last_state, grad_state))
    zeros_init = tuple((jnp.zeros_like(weight) for weight in params))
    grad_totals, row_results = lax.scan(row_step, zeros_init, (block_input, cotangent, init_state, doc_starts))
    outputs, grad_inputs, last_states, grad_states = row_results
    return (outputs, grad_inputs, last_states, grad_states, grad_totals[0], grad_totals[1], grad_totals[2], grad_totals[3], grad_totals[4], grad_totals[5], grad_totals[6], grad_totals[7], grad_totals[8], grad_totals[9])
```

```python
import functools

import jax
import jax.numpy as jnp
from jax import lax
from jax.experimental import pallas as pl
from jax.experimental.pallas import tpu as pltpu
from jax.sharding import PartitionSpec as P

GRAIN = 8
EPS = 1e-05
CORES = 2
F32 = jnp.float32
BF16 = jnp.bfloat16
MESH = pl.DeviceIdType.MESH
QUARTERS = 4
HALVES = 2
PARTS = 2
VMEM = pltpu.VMEM
ANY = pl.ANY
ROWS = 4
SMALLS = 4


def silu_slope(values):
    logistic = jax.nn.sigmoid(values)
    return logistic * (1.0 + values * (1.0 - logistic))


def enter(seq_count, batch_count, b, s):
    barrier = pltpu.get_barrier_semaphore()
    for i in range(1, seq_count):
        pl.semaphore_signal(
            barrier, inc=1, device_id=(b, lax.rem(s + i, seq_count)), device_id_type=MESH
        )
    for i in range(1, batch_count):
        pl.semaphore_signal(
            barrier, inc=1, device_id=(lax.rem(b + i, batch_count), s), device_id_type=MESH
        )
    pl.semaphore_wait(barrier, seq_count - 1 + batch_count - 1)


def remote(src, dst, send, recv, b, s):
    return pltpu.make_async_remote_copy(
        src_ref=src, dst_ref=dst, send_sem=send, recv_sem=recv, device_id=(b, s), device_id_type=MESH
    )


def strips(count, one, strip=16, first=0):
    def step(i, carry):
        one(pl.ds(pl.multiple_of(first + i * strip, strip), strip))
        return carry

    lax.fori_loop(0, count // strip, step, 0)


class LineGather:
    def __init__(self, S, b, s, src, out, sems):
        self.Z = S // CORES
        self.b, self.s, self.z, self.c = b, s, s // CORES, lax.rem(s, CORES)
        self.other = self.z * CORES + 1 - self.c
        self.src, self.out = src, out
        self.H = sems[0].shape[1]
        self.rows = src.shape[0] // self.H
        self.rs, self.rr, self.ls, self.lr, self.ss, self.sr = sems

    def piece(self, place, h):
        return self.out.at[place, pl.ds(h * self.rows, self.rows)]

    def own(self, h):
        return self.src.at[pl.ds(h * self.rows, self.rows)]

    def right(self, k, h):
        to = self.piece(self.s - CORES * k, h)
        return remote(
            self.own(h) if k == 0 else to, to, self.rs.at[k, h], self.rr.at[k, h], self.b, self.s + CORES
        )

    def left(self, k, h):
        to = self.piece(self.s + CORES * k, h)
        return remote(
            self.own(h) if k == 0 else to, to, self.ls.at[k, h], self.lr.at[k, h], self.b, self.s - CORES
        )

    def across(self, zz, h, mine=False):
        to = self.piece(zz * CORES + self.c, h)
        return remote(
            self.own(h) if mine else to, to, self.ss.at[zz, h], self.sr.at[zz, h], self.b, self.other
        )

    def arrived(self, place, h, sem):
        to = self.piece(place, h)
        remote(to, to, self.rs.at[0, h], sem, self.b, self.other).wait_recv()

    def start(self):
        for h in range(self.H):
            @pl.when(self.z + 1 < self.Z)
            def _():
                self.right(0, h).start()

            @pl.when(self.z > 0)
            def _():
                self.left(0, h).start()

            self.across(self.z, h, True).start()

    def relay(self, k, h):
        z, Z, s = self.z, self.Z, self.s

        @pl.when(z - k >= 0)
        def _():
            self.arrived(s - CORES * k, h, self.rr.at[k - 1, h])

            @pl.when(z + 1 < Z)
            def _():
                self.right(k, h).start()

            self.across(z - k, h).start()

        @pl.when(z + k < Z)
        def _():
            self.arrived(s + CORES * k, h, self.lr.at[k - 1, h])

            @pl.when(z > 0)
            def _():
                self.left(k, h).start()

            self.across(z + k, h).start()

    def drain(self):
        z, Z = self.z, self.Z
        for h in range(self.H):
            for k in range(Z):
                @pl.when((z - k >= 0) & (z + 1 < Z))
                def _():
                    self.right(k, h).wait_send()

                @pl.when((z + k < Z) & (z > 0))
                def _():
                    self.left(k, h).wait_send()

            for zz in range(Z):
                self.across(zz, h).wait_send()
                self.arrived(zz * CORES + 1 - self.c, h, self.sr.at[zz, h])


def line_gather_scratch(S, pieces):
    return [pltpu.SemaphoreType.DMA((S // CORES, pieces))] * 6


class LineSum:
    def __init__(self, S, b, s, src, acc, own, near, from_left, from_right, sems):
        self.Z = S // CORES
        self.b, self.z, self.c = b, s // CORES, lax.rem(s, CORES)
        self.s, self.sib = s, (s // CORES) * CORES + 1 - lax.rem(s, CORES)
        self.src, self.acc, self.own, self.near = src, acc, own, near
        self.from_left, self.from_right = from_left, from_right
        self.sib_s, self.sib_r, self.own_s, self.rs, self.rr, self.ls, self.lr = sems

    def sib_copy(self, zz):
        return remote(
            self.src.at[zz * CORES + 1 - self.c], self.near.at[zz], self.sib_s.at[zz],
            self.sib_r.at[zz], self.b, self.sib,
        )

    def own_copy(self, zz):
        return pltpu.make_async_copy(
            self.src.at[zz * CORES + self.c], self.own.at[zz], self.own_s.at[zz]
        )

    def half(self, h):
        rows = self.own.shape[1] // HALVES
        return pl.ds(h * rows, rows)

    def right(self, i, dest, h):
        at = self.half(h)
        return remote(
            self.own.at[dest, at], self.from_left.at[i, at], self.rs.at[i, h], self.rr.at[i, h],
            self.b, self.s + CORES,
        )

    def left(self, i, dest, h):
        at = self.half(h)
        return remote(
            self.own.at[dest, at], self.from_right.at[i, at], self.ls.at[i, h], self.lr.at[i, h],
            self.b, self.s - CORES,
        )

    def start(self):
        Z = self.Z

        def both(zz):
            self.sib_copy(zz).start()
            self.own_copy(zz).start()

        @pl.when(self.z == 0)
        def _():
            for j in range(Z):
                both(Z - 1 - j)

        @pl.when(self.z > 0)
        def _():
            for j in range(Z):
                both(j)

    def combine_one(self, zz):
        self.sib_copy(zz).wait_recv()
        self.own_copy(zz).wait()

        def one(at):
            total = self.own[zz, at].astype(F32) + self.near[zz, at].astype(F32)
            self.own[zz, at] = total.astype(BF16)

        strips(self.own.shape[1], one)

    def combine(self):
        Z = self.Z

        @pl.when(self.z == 0)
        def _():
            for j in range(Z):
                self.combine_one(Z - 1 - j)
                if j < Z - 1:
                    for h in range(HALVES):
                        self.right(j, Z - 1 - j, h).start()

        @pl.when(self.z > 0)
        def _():
            for j in range(Z):
                self.combine_one(j)
                if j < Z - 1:
                    @pl.when(self.z == Z - 1)
                    def _():
                        for h in range(HALVES):
                            self.left(j, j, h).start()

        def one(at):
            self.acc[at] = self.own[self.z, at].astype(F32)

        strips(self.own.shape[1], one)

    def take(self, buf, i, dest, last, h):
        rows = self.own.shape[1] // HALVES

        def one(at):
            if last:
                self.acc[at] = self.acc[at] + buf[i, at].astype(F32)
            else:
                total = self.own[dest, at].astype(F32) + buf[i, at].astype(F32)
                self.own[dest, at] = total.astype(BF16)

        strips(rows, one, 16, h * rows)

    def round(self, u, h):
        Z, z = self.Z, self.z

        @pl.when((z >= 1) & (z <= u))
        def _():
            i = u - z
            dest = Z - 1 - u + z
            self.right(i, dest, h).wait_recv()
            self.take(self.from_left, i, dest, u == Z - 1, h)
            if u < Z - 1:
                self.right(i, dest, h).start()

        @pl.when((z <= Z - 2) & (z >= Z - 1 - u))
        def _():
            i = u - (Z - 1) + z
            dest = u - (Z - 1) + z
            self.left(i, dest, h).wait_recv()
            self.take(self.from_right, i, dest, u == Z - 1, h)
            if u < Z - 1:
                self.left(i, dest, h).start()

    def drain(self):
        Z, z = self.Z, self.z
        for zz in range(Z):
            self.sib_copy(zz).wait_send()
        for i in range(Z - 1):
            @pl.when(i <= Z - 2 - z)
            def _():
                for h in range(HALVES):
                    self.right(i, Z - 1 - i, h).wait_send()

            @pl.when(i < z)
            def _():
                for h in range(HALVES):
                    self.left(i, i, h).wait_send()


def line_sum_scratch(S, rows, width):
    Z = S // CORES
    dma = pltpu.SemaphoreType.DMA
    return [
        VMEM((Z, rows, width), BF16), VMEM((Z, rows, width), BF16),
        VMEM((Z - 1, rows, width), BF16), VMEM((Z - 1, rows, width), BF16),
    ] + [dma((Z,))] * 3 + [dma((Z, HALVES))] * 4


class HomeSum:
    def __init__(self, B, S, b, s, src, out, buf, total, sems):
        self.B, self.S, self.b, self.s = B, S, b, s
        self.src, self.out, self.buf, self.total = src, out, buf, total
        self.s1, self.r1, self.s2, self.r2, self.loc = sems

    def first(self, j):
        bb = lax.rem(self.b + j, self.B)
        return remote(
            self.src.at[bb], self.buf.at[self.b], self.s1.at[j], self.r1.at[j], bb, self.s
        )

    def mine(self):
        return pltpu.make_async_copy(self.src.at[self.b], self.buf.at[self.b], self.loc.at[0])

    def lands(self):
        if self.out.ndim == 3:
            return [(slice(None), self.out.at[self.s])]
        B, S = self.B, self.S
        C = self.total.shape[2] // B
        return [
            (pl.ds(k * C, C), self.out.at[:, pl.ds(pl.multiple_of((k * S + self.s) * C, C), C)])
            for k in range(B)
        ]

    def second(self, i):
        ss = lax.rem(self.s + i, self.S)
        return [
            remote(
                self.total.at[ss, :, some], place, self.s2.at[i, k], self.r2.at[i, k], self.b, ss
            )
            for k, (some, place) in enumerate(self.lands())
        ]

    def start(self):
        for j in range(1, self.B):
            self.first(j).start()
        self.mine().start()

    def middle(self):
        self.mine().wait()
        for j in range(1, self.B):
            self.first(j).wait_recv()
        R = self.total.shape[1]

        def one(ss, carry):
            at = pl.ds(pl.multiple_of(ss * R, R), R)
            value = self.buf[0, at].astype(F32)
            for j in range(1, self.B):
                value = value + self.buf[j, at].astype(F32)
            self.total[ss] = value.astype(BF16)
            return carry

        lax.fori_loop(0, self.S, one, 0)
        for i in range(1, self.S):
            for copy in self.second(i):
                copy.start()
        for copy in self.kept():
            copy.start()

    def kept(self):
        return [
            pltpu.make_async_copy(self.total.at[self.s, :, some], place, self.loc.at[1 + k])
            for k, (some, place) in enumerate(self.lands())
        ]

    def drain(self):
        for copy in self.kept():
            copy.wait()
        for j in range(1, self.B):
            self.first(j).wait_send()
        for i in range(1, self.S):
            for copy in self.second(i):
                copy.wait()


def home_sum_scratch(B, S, shape):
    rows, width = shape
    dma = pltpu.SemaphoreType.DMA
    return [
        VMEM((B, rows, width), BF16), VMEM((S, rows // S, width), BF16),
        dma((B,)), dma((B,)), dma((S, B)), dma((S, B)), dma((1 + B,)),
    ]


def home_sum_shape(B, S, shape):
    rows, width = shape
    if (width // B) % 128 == 0:
        return jax.ShapeDtypeStruct((rows // S, S * width), BF16)
    return jax.ShapeDtypeStruct((S, rows // S, width), BF16)


def gather_kernel(
    B, S, made, x_ref, w_ref, g_ref, *refs
):
    smalls, refs = refs[: SMALLS - 1], refs[SMALLS - 1 :]
    rows, refs = refs[:ROWS], refs[ROWS:]
    xg_ref, wf_ref, refs = refs[0], refs[1], refs[2:]
    smalls_out, refs = refs[:SMALLS], refs[SMALLS:]
    xh_ref, wp_ref, tail_ref, w1s, w1r, w2s, w2r, ps, pr, loc, *line_sems = refs
    Z = S // CORES
    b = lax.axis_index("batch")
    s = lax.axis_index("seq")
    line = LineGather(S, b, s, xh_ref, xg_ref, line_sems)
    values = [row[...].astype(F32) for row in rows]
    free = tail_ref.shape[0] - sum(value.shape[0] for value in values)
    values.append(jnp.zeros((free, tail_ref.shape[1]), F32))
    tail_ref[...] = jnp.concatenate(values, axis=0).astype(BF16)
    smalls = smalls + (tail_ref,)
    if made:
        R, C = w_ref.shape[0], w_ref.shape[1] // (2 * B * S)

        def one(at):
            rows = w_ref[at].astype(F32) * g_ref[at]
            for place in range(2 * B):
                for to in range(S):
                    first = (place * S + to) * C
                    wp_ref[to, at, place * C : place * C + C] = rows[:, first : first + C].astype(BF16)

        strips(R, one)
        w_ref = wp_ref
    enter(S, B, b, s)

    def batch_copy(i, j):
        src_s = lax.rem(s + S - i, S)
        src = w_ref.at[s] if i == 0 else wf_ref.at[b, src_s]
        return remote(
            src, wf_ref.at[b, src_s], w2s.at[j - 1, i], w2r.at[j - 1, i], lax.rem(b + j, B), s
        )

    def seq_copy(i):
        dst_s = lax.rem(s + i, S)
        return remote(w_ref.at[dst_s], wf_ref.at[b, s], w1s.at[i], w1r.at[i], b, dst_s)

    def small_copy(n, j):
        return remote(
            smalls[n], smalls_out[n].at[b], ps.at[n, j - 1], pr.at[n, j - 1], lax.rem(b + j, B), s
        )

    for i in range(1, S):
        seq_copy(i).start()
    for j in range(1, B):
        for n in range(SMALLS):
            small_copy(n, j).start()
    for j in range(1, B):
        batch_copy(0, j).start()

    def norm(at):
        x = x_ref[at].astype(F32)
        xh_ref[at] = (x * lax.rsqrt(jnp.mean(x * x, axis=-1, keepdims=True) + EPS)).astype(BF16)

    strips(x_ref.shape[0], norm)

    line.start()
    locals_ = [
        pltpu.make_async_copy(xh_ref, xg_ref.at[s], loc.at[0]),
        pltpu.make_async_copy(w_ref.at[s], wf_ref.at[b, s], loc.at[1]),
    ] + [
        pltpu.make_async_copy(smalls[n], smalls_out[n].at[b], loc.at[2 + n]) for n in range(SMALLS)
    ]
    for copy in locals_:
        copy.start()

    for i in range(1, S):
        seq_copy(i).wait_recv()
        for j in range(1, B):
            batch_copy(i, j).start()

    for k in range(1, Z):
        for h in range(QUARTERS):
            line.relay(k, h)

    line.drain()
    for i in range(1, S):
        seq_copy(i).wait_send()
    for i in range(S):
        src_s = lax.rem(s + S - i, S)
        for j in range(1, B):
            src_b = lax.rem(b + B - j, B)
            batch_copy(i, j).wait_send()
            remote(
                wf_ref.at[src_b, src_s], wf_ref.at[src_b, src_s],
                w2s.at[j - 1, i], w2r.at[j - 1, i], src_b, s,
            ).wait_recv()
    for j in range(1, B):
        src_b = lax.rem(b + B - j, B)
        for n in range(SMALLS):
            small_copy(n, j).wait_send()
            place = smalls_out[n].at[src_b]
            remote(place, place, ps.at[n, j - 1], pr.at[n, j - 1], src_b, s).wait_recv()
    for copy in locals_:
        copy.wait()


def gather_all(B, S, x, weight, gain, smalls, rows):
    Z = S // CORES
    R, E = weight.shape
    C = E // (2 * B * S)
    made = C % 128 == 0 and R % 16 == 0
    if not made:
        weight = (weight.astype(F32) * gain).astype(BF16).reshape(R, 2 * B, S, C)
        weight = weight.transpose(2, 0, 1, 3).reshape(S, R, E // S)
    dma = pltpu.SemaphoreType.DMA
    return pl.pallas_call(
        functools.partial(gather_kernel, B, S, made),
        out_shape=(
            jax.ShapeDtypeStruct((S,) + x.shape, BF16),
            jax.ShapeDtypeStruct((B, S, R, E // S), BF16),
        ) + tuple(jax.ShapeDtypeStruct((B,) + small.shape, BF16) for small in smalls)
        + (jax.ShapeDtypeStruct((B, 16, rows[0].shape[1]), BF16),),
        in_specs=[pl.BlockSpec(memory_space=VMEM)] * (2 + SMALLS + ROWS),
        out_specs=(pl.BlockSpec(memory_space=ANY),) * (2 + SMALLS),
        scratch_shapes=[
            VMEM(x.shape, BF16), VMEM((S, R, E // S), BF16), VMEM((16, rows[0].shape[1]), BF16),
            dma((S,)), dma((S,)), dma((B - 1, S)), dma((B - 1, S)),
            dma((SMALLS, B - 1)), dma((SMALLS, B - 1)), dma((2 + SMALLS,)),
        ]
        + line_gather_scratch(S, QUARTERS),
        compiler_params=pltpu.CompilerParams(collective_id=1, has_side_effects=True),
        name="gather_all",
    )(x, weight, gain, *smalls, *rows)


def token_sums(parts):
    width = parts[0].shape[1]
    row = lax.broadcasted_iota(jnp.int32, (8, width), 0)
    for bit in (1, 2, 4):
        low = (row & bit) == 0
        merged = []
        for k in range(0, len(parts), 2):
            first, second = parts[k], parts[k + 1]
            merged.append(
                jnp.where(low, first, second) + pltpu.roll(jnp.where(low, second, first), bit, 0)
            )
        parts = merged
    return parts[0]


def forward_kernel(
    B, S, groups, N, keep_ref, part_ref, act_ref, dtproj_ref, bias_ref, rate_ref, init_ref, cot_ref,
    ow_ref,
    read_ref, hs_ref, last_ref, step_out, pre_out, rank_out, coef_out, cots_ref, ows_ref,
    h_ref, act_f32, terms, ranks, coefs, p_s, p_r, rank_s, rank_r, coef_s, coef_r,
    ow_s, ow_r, loc, *line_sems,
):
    rank = ranks.shape[1]
    block = pl.program_id(0)
    width = groups * GRAIN
    Z = S // CORES
    b = lax.axis_index("batch")
    s = lax.axis_index("seq")
    line = LineGather(S, b, s, cot_ref, cots_ref, line_sems)

    def ow_copy(j):
        return remote(ow_ref, ows_ref.at[b], ow_s.at[j], ow_r.at[j], lax.rem(b + j, B), s)

    def mine():
        return [
            pltpu.make_async_copy(cot_ref, cots_ref.at[s], loc.at[0]),
            pltpu.make_async_copy(ow_ref, ows_ref.at[b], loc.at[1]),
        ]

    def term_copy(i):
        return remote(part_ref.at[i], terms.at[s], p_s.at[i], p_r.at[s], b, i)

    def sum_copies(to, source):
        return [
            remote(ranks.at[source], ranks.at[source], rank_s.at[to], rank_r.at[source], b, to),
            remote(coefs.at[source], coefs.at[source], coef_s.at[to], coef_r.at[source], b, to),
        ]

    @pl.when(block == 0)
    def _():
        h_ref[...] = init_ref[...]
        enter(S, B, b, s)
        for i in range(S):
            @pl.when(s != i)
            def _():
                term_copy(i).start()

        total = part_ref[s].astype(F32)
        for i in range(1, S):
            source = lax.rem(s + i, S)
            remote(part_ref.at[s], terms.at[source], p_s.at[0], p_r.at[source], b, source).wait_recv()
            total = total + terms[source].astype(F32)
        ranks[s] = total[:rank].astype(BF16)
        coefs[s] = total[rank:]
        for i in range(S):
            @pl.when(s != i)
            def _():
                for copy in sum_copies(i, s):
                    copy.start()

        line.start()
        for j in range(1, B):
            ow_copy(j).start()
        for copy in mine():
            copy.start()

    for k in range(1, Z):
        for h in range(HALVES):
            if HALVES * k + h < S - 1:
                @pl.when(block == HALVES * k + h)
                def _():
                    line.relay(k, h)

    @pl.when(s != block)
    def _():
        for copy in sum_copies(block, block):
            copy.wait_recv()

    here = ranks[block]
    coef_here = coefs[block]
    rank_out[0] = here
    coef_out[0] = coef_here
    pre = lax.dot_general(here, dtproj_ref[...], (((0,), (0,)), ((), ())), preferred_element_type=F32)
    pre = pre + bias_ref[...]
    pre_out[0] = pre
    step_out[0] = jnp.maximum(pre, 0.0) + jnp.log1p(jnp.exp(-jnp.abs(pre)))
    act_f32[...] = act_ref[0].astype(F32)
    rate = rate_ref[...]

    def group(g, h):
        at = pl.multiple_of(g * GRAIN, GRAIN)
        coef = pltpu.roll(coef_here, lax.rem(width - at, width), 1)
        step = step_out[0, pl.ds(at, GRAIN), :]
        drive = step * act_f32[pl.ds(at, GRAIN), :]
        h = h * keep_ref[block * groups + g]
        parts = []
        for j in range(GRAIN):
            decay = jnp.exp(step[j : j + 1] * rate)
            h = decay * h + coef[:N, j : j + 1] * drive[j : j + 1]
            hs_ref[0, at + j] = h
            seen = coef[N:, j : j + 1] * h
            parts.append(seen[:8] + seen[8:])
        read_ref[0, pl.ds(at, GRAIN), :] = token_sums(parts)
        return h

    h = lax.fori_loop(0, groups, group, h_ref[...])
    h_ref[...] = h
    last_ref[...] = h

    @pl.when(block == S - 1)
    def _():
        for k in range(1, Z):
            for h in range(HALVES):
                if HALVES * k + h >= S - 1:
                    line.relay(k, h)
        for i in range(S):
            @pl.when(s != i)
            def _():
                term_copy(i).wait_send()
                for copy in sum_copies(i, s):
                    copy.wait_send()

        line.drain()
        for j in range(1, B):
            source = lax.rem(b + B - j, B)
            ow_copy(j).wait_send()
            remote(ows_ref.at[source], ows_ref.at[source], ow_s.at[j], ow_r.at[j], source, s).wait_recv()
        for copy in mine():
            copy.wait()


def scan_forward(B, keep, part, act, dtproj, bias, rate, init, cot, ow):
    S, width, inner = act.shape
    N = rate.shape[0]
    rank = dtproj.shape[0]
    groups = width // GRAIN
    Z = S // CORES
    token = pl.BlockSpec((1, width, inner), lambda i: (i, 0, 0))
    whole = pl.BlockSpec(memory_space=VMEM)
    hbm = pl.BlockSpec(memory_space=ANY)
    state = pl.BlockSpec((N, inner), lambda i: (0, 0))
    dma = pltpu.SemaphoreType.DMA
    tokens = jax.ShapeDtypeStruct((S, width, inner), F32)
    return pl.pallas_call(
        functools.partial(forward_kernel, B, S, groups, N),
        grid=(S,),
        out_shape=(
            tokens,
            jax.ShapeDtypeStruct((S, width, N, inner), F32),
            jax.ShapeDtypeStruct((N, inner), F32),
            tokens,
            tokens,
            jax.ShapeDtypeStruct((S, rank, width), BF16),
            jax.ShapeDtypeStruct((S, 2 * N, width), F32),
            jax.ShapeDtypeStruct((S,) + cot.shape, BF16),
            jax.ShapeDtypeStruct((B,) + ow.shape, BF16),
        ),
        in_specs=[
            pl.BlockSpec(memory_space=pltpu.SMEM), whole, token, whole, whole, state, state, whole, whole,
        ],
        out_specs=(
            token, pl.BlockSpec((1, width, N, inner), lambda i: (i, 0, 0, 0)), state, token, token,
            pl.BlockSpec((1, rank, width), lambda i: (i, 0, 0)),
            pl.BlockSpec((1, 2 * N, width), lambda i: (i, 0, 0)),
            hbm, hbm,
        ),
        scratch_shapes=[
            VMEM((N, inner), F32), VMEM((width, inner), F32), VMEM(part.shape, BF16),
            VMEM((S, rank, width), BF16), VMEM((S, 2 * N, width), F32),
            dma((S,)), dma((S,)), dma((S,)), dma((S,)), dma((S,)), dma((S,)),
            dma((B,)), dma((B,)), dma((2,)),
        ]
        + line_gather_scratch(S, HALVES),
        compiler_params=pltpu.CompilerParams(collective_id=5, has_side_effects=True),
        name="scan_forward",
    )(keep, part, act, dtproj, bias, rate, init, cot, ow)


def backward_kernel(
    B, S, groups, N, keep_ref, step_ref, pre_ref, act_ref, pull_ref, coef_ref, hs_ref, before_ref,
    rate_ref, init_ref, dtproj_ref, op_ref, dg_ref, og_ref,
    step_low_ref, act_grad_ref, decay_ref, start_ref, bias_ref, bo_ref, dgo_ref, ogs_ref, proj_ref,
    g_ref, prior_ref, act_f32, step_grad, sends, near, mid, terms, fin,
    a_s, a_r, t_s, t_r, f_s, f_r, own, og_s, og_r, og_own, *scratch,
):
    turn = pl.program_id(0)
    block = pl.num_programs(0) - 1 - turn
    width = groups * GRAIN
    b = lax.axis_index("batch")
    s = lax.axis_index("seq")
    line = LineSum(S, b, s, op_ref, bo_ref, *scratch[:4], scratch[4:11])
    home = HomeSum(B, S, b, s, dg_ref, dgo_ref, *scratch[11:13], scratch[13:])

    def og_copy(j):
        bb = lax.rem(b + j, B)
        return remote(og_ref.at[bb], ogs_ref.at[b], og_s.at[j], og_r.at[j], bb, s)

    def og_keep():
        return pltpu.make_async_copy(og_ref.at[b], ogs_ref.at[b], og_own.at[0])

    Z = S // CORES
    z = s // CORES
    c = lax.rem(s, CORES)
    sib = z * CORES + 1 - c

    def half_copy(i):
        return remote(sends.at[i, 1 - c], near.at[i], a_s.at[i], a_r.at[i], b, sib)

    def chip_copy(i, k):
        to = lax.rem(z + k, Z)
        return remote(
            mid.at[i], terms.at[i, z], t_s.at[k, i], t_r.at[k, i], b, to * CORES + c
        )

    def final_copy(i):
        return remote(fin.at[i], proj_ref.at[i, c], f_s.at[i], f_r.at[i], b, sib)

    def final_keep(i):
        return pltpu.make_async_copy(fin.at[i], proj_ref.at[i, c], own.at[i])

    def over_cores(i):
        half_copy(i).wait_recv()
        mid[i] = (sends[i, c].astype(F32) + near[i].astype(F32)).astype(BF16)
        for k in range(1, Z):
            chip_copy(i, k).start()

    def over_chips(i):
        value = mid[i].astype(F32)
        for k in range(1, Z):
            chip_copy(i, k).wait_recv()
            value = value + terms[i, lax.rem(z + Z - k, Z)].astype(F32)
        fin[i] = value.astype(BF16)
        final_copy(i).start()
        final_keep(i).start()

    @pl.when(turn == 0)
    def _():
        g_ref[...] = jnp.zeros_like(g_ref)
        decay_ref[...] = jnp.zeros_like(decay_ref)
        bias_ref[...] = jnp.zeros_like(bias_ref)
        enter(S, B, b, s)
        line.start()
        home.start()
        for j in range(1, B):
            og_copy(j).start()
        og_keep().start()

    @pl.when(turn == 1)
    def _():
        line.combine()

    for u in range(1, S // CORES):
        for h in range(HALVES):
            @pl.when(turn == HALVES * u + h)
            def _():
                line.round(u, h)

    @pl.when(turn == S - 2)
    def _():
        home.middle()

    @pl.when(turn >= 2)
    def _():
        over_cores(S + 1 - turn)


    act_f32[...] = act_ref[0].astype(F32)

    prior_ref[...] = jnp.where(block > 0, before_ref[0, 0], init_ref[...])
    inner = step_ref.shape[2]
    lane = lax.broadcasted_iota(jnp.int32, (2 * N, width), 1)

    parts = PARTS if inner % (PARTS * 128) == 0 else 1
    lanes = [pl.ds(i * (inner // parts), inner // parts) for i in range(parts)]

    def fold(value):
        count = value.shape[1] // 128
        return sum((value[:, i * 128 : (i + 1) * 128] for i in range(1, count)), value[:, :128])

    def group(k, carry):
        states, coef_grad = carry
        g = groups - 1 - k
        at = pl.multiple_of(g * GRAIN, GRAIN)
        coef = pltpu.roll(coef_ref[0], lax.rem(width - at, width), 1)
        keep = keep_ref[block * groups + g]
        after = []
        entries = [0.0] * GRAIN
        leaves = [0.0] * GRAIN
        for (carried, total), some in zip(states, lanes):
            step = step_ref[0, pl.ds(at, GRAIN), some]
            act = act_f32[pl.ds(at, GRAIN), some]
            pull = pull_ref[0, pl.ds(at, GRAIN), some]
            rate = rate_ref[:, some]
            drive = step * act
            rate_parts = [None] * GRAIN
            drive_parts = [None] * GRAIN
            for j in reversed(range(GRAIN)):
                step_j = step[j : j + 1]
                decay = jnp.exp(step_j * rate)
                costate = coef[N:, j : j + 1] * pull[j : j + 1] + carried
                carried = decay * costate
                if j == 0:
                    prior = jnp.where(
                        g > 0, hs_ref[0, jnp.maximum(at - 1, 0), :, some], prior_ref[:, some]
                    ) * keep
                else:
                    prior = hs_ref[0, at + j - 1, :, some]
                rate_grad = carried * prior
                if j == 0:
                    carried = carried * keep
                total = total + rate_grad * step_j
                part = rate_grad * rate
                rate_parts[j] = part[:8] + part[8:]
                part = costate * coef[:N, j : j + 1]
                drive_parts[j] = part[:8] + part[8:]
                entries[j] = entries[j] + fold(costate * drive[j : j + 1])
                leaves[j] = leaves[j] + fold(hs_ref[0, at + j, :, some] * pull[j : j + 1])
            drive_pull = token_sums(drive_parts)
            step_grad[pl.ds(at, GRAIN), some] = token_sums(rate_parts) + drive_pull * act
            act_grad_ref[0, pl.ds(at, GRAIN), some] = drive_pull * step
            after.append((carried, total))
        for j in range(GRAIN):
            both = jnp.sum(jnp.concatenate([entries[j], leaves[j]], axis=0), axis=1, keepdims=True)
            coef_grad = jnp.where(lane == at + j, both, coef_grad)
        return tuple(after), coef_grad

    states, coef_grad = lax.fori_loop(
        0, groups, group,
        (
            tuple((g_ref[:, some], decay_ref[:, some]) for some in lanes),
            jnp.zeros((2 * N, width), F32),
        ),
    )
    carried = jnp.concatenate([state[0] for state in states], axis=1)
    total = jnp.concatenate([state[1] for state in states], axis=1)
    g_ref[...] = carried
    start_ref[...] = carried
    decay_ref[...] = total
    pre_grad = step_grad[...] * jax.nn.sigmoid(pre_ref[0])
    bias_ref[...] = bias_ref[...] + jnp.sum(pre_grad, axis=0, keepdims=True)
    low = pre_grad.astype(BF16)
    step_low_ref[0] = low
    rank_grad = lax.dot_general(
        dtproj_ref[...], low, (((1,), (1,)), ((), ())), preferred_element_type=F32
    )
    low = jnp.concatenate([rank_grad, coef_grad], axis=0).astype(BF16)
    rows = sends.shape[2]
    for half in range(CORES):
        sends[block, half] = low[half * rows : (half + 1) * rows]
    half_copy(block).start()

    @pl.when(turn == S - 1)
    def _():
        over_cores(1)
        over_cores(0)
        line.drain()
        home.drain()
        for i in reversed(range(S)):
            over_chips(i)
        for i in range(S):
            half_copy(i).wait_send()
            for k in range(1, Z):
                chip_copy(i, k).wait_send()
            final_copy(i).wait_send()
            remote(fin.at[i], proj_ref.at[i, 1 - c], f_s.at[i], f_r.at[i], b, sib).wait_recv()
            final_keep(i).wait()
        og_keep().wait()
        for j in range(1, B):
            source = lax.rem(b + B - j, B)
            og_copy(j).wait_send()
            remote(ogs_ref.at[source], ogs_ref.at[source], og_s.at[j], og_r.at[j], source, s).wait_recv()


def scan_backward(B, keep, step, pre, act, pull, coef, hs, rate, init, dtproj, op, dg, og):
    S, width, inner = step.shape
    N = rate.shape[0]
    rank = dtproj.shape[0]
    groups = width // GRAIN
    token = pl.BlockSpec((1, width, inner), lambda i: (S - 1 - i, 0, 0))
    coefs = pl.BlockSpec((1, 2 * N, width), lambda i: (S - 1 - i, 0, 0))
    state = pl.BlockSpec((N, inner), lambda i: (0, 0))
    whole = pl.BlockSpec(memory_space=VMEM)
    hbm = pl.BlockSpec(memory_space=ANY)
    dma = pltpu.SemaphoreType.DMA
    half = ((rank + 2 * N) // CORES, width)
    Z = S // CORES
    return pl.pallas_call(
        functools.partial(backward_kernel, B, S, groups, N),
        grid=(S,),
        out_shape=(
            jax.ShapeDtypeStruct((S, width, inner), BF16),
            jax.ShapeDtypeStruct((S, width, inner), F32),
            jax.ShapeDtypeStruct((N, inner), F32),
            jax.ShapeDtypeStruct((N, inner), F32),
            jax.ShapeDtypeStruct((1, inner), F32),
            jax.ShapeDtypeStruct(op.shape[1:], F32),
            home_sum_shape(B, S, dg.shape[1:]),
            jax.ShapeDtypeStruct(og.shape, BF16),
            jax.ShapeDtypeStruct((S, CORES) + half, BF16),
        ),
        in_specs=[
            pl.BlockSpec(memory_space=pltpu.SMEM), token, token, token, token, coefs,
            pl.BlockSpec((1, width, N, inner), lambda i: (S - 1 - i, 0, 0, 0)),
            pl.BlockSpec(
                (1, 1, N, inner), lambda i: (jnp.maximum(S - 2 - i, 0), width - 1, 0, 0)
            ),
            state, state, whole, hbm, hbm, hbm,
        ],
        out_specs=(
            token, token, state, state, pl.BlockSpec((1, inner), lambda i: (0, 0)), whole, hbm, hbm, hbm,
        ),
        scratch_shapes=[
            VMEM((N, inner), F32), VMEM((N, inner), F32), VMEM((width, inner), F32),
            VMEM((width, inner), F32), VMEM((S, CORES) + half, BF16), VMEM((S,) + half, BF16),
            VMEM((S,) + half, BF16), VMEM((S, Z) + half, BF16), VMEM((S,) + half, BF16),
            dma((S,)), dma((S,)), dma((Z, S)), dma((Z, S)), dma((S,)), dma((S,)), dma((S,)),
            dma((B,)), dma((B,)), dma((1,)),
        ]
        + line_sum_scratch(S, *op.shape[1:])
        + home_sum_scratch(B, S, dg.shape[1:]),
        compiler_params=pltpu.CompilerParams(collective_id=6, has_side_effects=True),
        name="scan_backward",
    )(keep, step, pre, act, pull, coef, hs, hs, rate, init, dtproj, op, dg, og)


def columns(ref, i, width):
    if ref.ndim == 3:
        return ref.at[i]
    return ref.at[:, pl.ds(pl.multiple_of(i * width, width), width)]


def scatter_kernel(B, S, count, C, dx_ref, dw_ref, st_ref, *refs):
    grads, refs = refs[:count], refs[count:]
    dxo_ref, dwo_ref, sto_ref, refs = refs[0], refs[1], refs[2], refs[3:]
    sums, refs = refs[:count], refs[count:]
    bufs, refs = refs[:count], refs[count:]
    g_s, g_r, st_s, st_r, loc, *scratch = refs
    b = lax.axis_index("batch")
    s = lax.axis_index("seq")
    line = LineSum(S, b, s, dx_ref, dxo_ref, *scratch[:4], scratch[4:11])
    home = HomeSum(B, S, b, s, dw_ref, dwo_ref, *scratch[11:13], scratch[13:])
    enter(S, B, b, s)

    def grad_copy(n, j):
        bb = lax.rem(b + j, B)
        return remote(
            columns(grads[n], bb, C), bufs[n].at[b], g_s.at[n, j], g_r.at[n, j], bb, s
        )

    def grad_here(n):
        return pltpu.make_async_copy(columns(grads[n], b, C), bufs[n].at[b], loc.at[n])

    def st_place(j):
        place = j * S + s
        return place // B, lax.rem(place, B)

    def st_copy(j):
        to, slot = st_place(j)
        return remote(
            columns(st_ref, j, C), columns(sto_ref, slot, C), st_s.at[j], st_r.at[slot], b, to
        )

    def st_local(j):
        to, slot = st_place(j)
        return pltpu.make_async_copy(columns(st_ref, j, C), columns(sto_ref, slot, C), st_s.at[j])

    line.start()
    home.start()
    for n in range(count):
        for j in range(1, B):
            grad_copy(n, j).start()
        grad_here(n).start()
    for j in range(B):
        to, slot = st_place(j)

        @pl.when(to != s)
        def _():
            st_copy(j).start()

        @pl.when(to == s)
        def _():
            st_local(j).start()

    Z = S // CORES
    line.combine()
    for u in range(1, Z):
        for h in range(HALVES):
            line.round(u, h)
        if u == max(Z - 2, 1):
            home.middle()
    for n in range(count):
        grad_here(n).wait()
        for j in range(1, B):
            source = lax.rem(b + B - j, B)
            place = bufs[n].at[source]
            remote(place, place, g_s.at[n, j], g_r.at[n, j], source, s).wait_recv()
        total = bufs[n][0]
        for j in range(1, B):
            total = total + bufs[n][j]
        sums[n][...] = total

    line.drain()
    home.drain()
    for n in range(count):
        for j in range(1, B):
            grad_copy(n, j).wait_send()
    for j in range(B):
        to, slot = st_place(j)

        @pl.when(to != s)
        def _():
            st_copy(j).wait_send()

        @pl.when(to == s)
        def _():
            st_local(j).wait()

    for slot in range(B):
        source = lax.rem(s * B + slot, S)

        @pl.when(source != s)
        def _():
            place = columns(sto_ref, slot, C)
            remote(place, place, st_s.at[0], st_r.at[slot], b, source).wait_recv()


def scatter_all(B, S, dx, dw, st, grads):
    _, rows, D = dx.shape
    inner = dw.shape[2]
    C = inner // B
    if C % 128:

        def parts(value):
            return value.reshape(value.shape[0], B, C).transpose(1, 0, 2)

        st, grads = parts(st), [parts(grad) for grad in grads]
    dma = pltpu.SemaphoreType.DMA
    count = len(grads)
    heights = [grad.shape[-2] for grad in grads]
    return pl.pallas_call(
        functools.partial(scatter_kernel, B, S, count, C),
        out_shape=(
            jax.ShapeDtypeStruct((rows, D), F32),
            home_sum_shape(B, S, dw.shape[1:]),
            jax.ShapeDtypeStruct(st.shape, F32),
        ) + tuple(jax.ShapeDtypeStruct((height, C), F32) for height in heights),
        in_specs=[pl.BlockSpec(memory_space=ANY)] * (3 + count),
        out_specs=(pl.BlockSpec(memory_space=VMEM),) * (3 + count),
        scratch_shapes=[VMEM((B, height, C), F32) for height in heights]
        + [dma((count, B)), dma((count, B)), dma((B,)), dma((B,)), dma((count,))]
        + line_sum_scratch(S, rows, D)
        + home_sum_scratch(B, S, dw.shape[1:]),
        compiler_params=pltpu.CompilerParams(collective_id=4, has_side_effects=True),
        name="scatter_all",
    )(dx, dw, st, *grads)


def body(
    B, S,
    block_input, cotangent, init_state, doc_starts, norm_gain, in_weight, conv_weight, conv_bias,
    xproj_weight, dtproj_weight, dt_bias, decay_log, skip_gain, out_weight,
):
    _, width, D = block_input.shape
    T = S * width
    R = in_weight.shape[0]
    C = conv_bias.shape[0]
    inner = B * C
    taps = conv_weight.shape[0]
    rank = dtproj_weight.shape[0]
    N = decay_log.shape[0]
    s = lax.axis_index("seq")

    x = block_input[0].astype(F32)
    inv_rms = lax.rsqrt(jnp.mean(x * x, axis=-1, keepdims=True) + EPS)
    xhat = (x * inv_rms).astype(BF16)
    gain = norm_gain.astype(F32)[:, None]
    weight_rows = in_weight.astype(F32)
    rows = [
        dtproj_weight, xproj_weight.T, decay_log, conv_weight,
        conv_bias[None], dt_bias[None], skip_gain[None],
    ]
    xg, wf, *smalls = gather_all(B, S, block_input[0], in_weight, gain, rows[:3], rows[3:])
    tokens = xg.reshape(T, D)
    full_in = wf.reshape(D, 2 * inner)
    dtproj, xproj_t, decay_full, tail = (
        small.transpose(1, 0, 2).reshape(small.shape[1], inner) for small in smalls
    )
    conv_full, conv_b, dt_b, skip = (
        tail[:taps], tail[taps : taps + 1], tail[taps + 1 : taps + 2], tail[taps + 2 : taps + 3]
    )
    conv_full = conv_full.astype(F32)
    skip = skip.astype(F32)

    places = jnp.arange(T, dtype=jnp.int32)
    starts = doc_starts[0]

    def doc_number(at):
        return jnp.sum((at[:, None] >= starts[None, :]).astype(jnp.int32), axis=1)

    doc_here = doc_number(places)
    masks = [
        (doc_number(places - (taps - 1 - tap)) == doc_here).astype(F32)[:, None]
        for tap in range(taps)
    ]
    heads = GRAIN * jnp.arange(T // GRAIN, dtype=jnp.int32)
    keep = 1.0 - jnp.any(heads[:, None] == starts[None, :], axis=1).astype(F32)

    mixed = jnp.dot(tokens, full_in, preferred_element_type=F32)
    conv_in = mixed[:, :inner].astype(BF16)
    gate_pre = mixed[:, inner:]
    extended = jnp.pad(conv_in, ((taps - 1, 0), (0, 0))).astype(F32)
    conv_out = jnp.zeros((T, inner), F32) + conv_b.astype(F32)
    for tap in range(taps):
        conv_out = conv_out + conv_full[tap] * extended[tap : tap + T] * masks[tap]
    act_in = jax.nn.silu(conv_out).astype(BF16)
    act = act_in.astype(F32)

    part = lax.dot_general(xproj_t, act_in, (((1,), (1,)), ((), ())), preferred_element_type=F32)
    part = part.astype(BF16).reshape(-1, S, width).transpose(1, 0, 2)
    rate = -jnp.exp(decay_full.astype(F32))
    start = init_state[0].reshape(N, B, S, C)
    start = lax.dynamic_index_in_dim(start, s, 2, False).reshape(N, inner)
    act3 = act_in.reshape(S, width, inner)
    readout, hs, last, step, step_pre, rank_in, coef, cot, full_out = scan_forward(
        B, keep, part, act3, dtproj, dt_b.astype(F32), rate, start, cotangent[0], out_weight
    )
    cot = cot.reshape(T, D)
    full_out = full_out.reshape(inner, D)

    mixed_out = readout.reshape(T, inner) + skip * act
    gate_act = jax.nn.silu(gate_pre)
    gated_out = (mixed_out * gate_act).astype(BF16)
    out_part = jnp.dot(gated_out, full_out, preferred_element_type=F32)
    out_part = out_part.astype(BF16).reshape(S, width, D)

    gated_grad = lax.dot_general(cot, full_out, (((1,), (1,)), ((), ())), preferred_element_type=F32)
    mixer_grad = gated_grad * gate_act
    gate_low = (gated_grad * mixed_out * silu_slope(gate_pre)).astype(BF16)
    skip_grad = jnp.sum(mixer_grad * act, axis=0)
    out_grad_part = lax.dot_general(
        gated_out, cot, (((0,), (0,)), ((), ())), preferred_element_type=F32
    )
    out_grad_part = out_grad_part.astype(BF16).reshape(B, C, D)
    dw_gate = lax.dot_general(tokens, gate_low, (((0,), (0,)), ((), ())), preferred_element_type=F32)
    dw_gate = dw_gate.astype(BF16).reshape(B, S * R, inner)

    step_low, act_grad, decay_grad, start_grad, dt_bias_grad, out_sum, dwo_gate, terms, proj_grad = (
        scan_backward(
            B, keep, step, step_pre, act3, mixer_grad.reshape(S, width, inner), coef, hs, rate, start,
            dtproj, out_part, dw_gate, out_grad_part,
        )
    )
    proj_grad = proj_grad.reshape(S, rank + 2 * N, width)
    block_output = (x + out_sum).astype(BF16)[None]
    out_weight_grad = jnp.sum(terms.astype(F32), axis=0)
    decay_log_grad = decay_grad * rate
    dtproj_grad = jnp.einsum("skt,std->kd", rank_in, step_low, preferred_element_type=F32)
    xproj_grad = jnp.einsum(
        "set,std->ed", proj_grad, act3, preferred_element_type=F32
    )
    act_total = (
        act_grad.reshape(T, inner)
        + mixer_grad * skip
        + jnp.einsum("set,ed->std", proj_grad, xproj_t, preferred_element_type=F32).reshape(T, inner)
    )
    conv_grad = act_total * silu_slope(conv_out)
    conv_bias_grad = jnp.sum(conv_grad, axis=0)
    tap_grads = []
    conv_in_grad = jnp.zeros((T, inner), F32)
    for tap in range(taps):
        masked = conv_grad * masks[tap]
        tap_grads.append(jnp.sum(masked * extended[tap : tap + T], axis=0))
        back = taps - 1 - tap
        conv_in_grad = conv_in_grad + jnp.pad(conv_full[tap] * masked, ((0, back), (0, 0)))[back:]
    conv_low = conv_in_grad.astype(BF16)
    mixed_grad = jnp.concatenate([conv_low, gate_low], axis=-1)

    dw = lax.dot_general(tokens, conv_low, (((0,), (0,)), ((), ())), preferred_element_type=F32)
    dw = dw.astype(BF16).reshape(B, S * R, inner)
    dx = lax.dot_general(mixed_grad, full_in, (((1,), (1,)), ((), ())), preferred_element_type=F32)
    dx = dx.astype(BF16).reshape(S, width, D)
    misc = jnp.concatenate(
        [jnp.stack(tap_grads), conv_bias_grad[None], dt_bias_grad, skip_grad[None]]
        + [jnp.zeros((-(taps + 3) % 8, inner), F32)],
        axis=0,
    )
    gained, dwo, states, dtproj_g, xproj_g, decay_g, misc = scatter_all(
        B, S, dx, dw, jnp.concatenate([last, start_grad], axis=0),
        [dtproj_grad, xproj_grad, decay_log_grad, misc],
    )
    if states.ndim == 3:
        states = states.transpose(1, 0, 2).reshape(2 * N, inner)
    input_grad = (
        cotangent[0].astype(F32)
        + inv_rms * gained
        - x * inv_rms * inv_rms * inv_rms * jnp.mean(gained * x, axis=-1, keepdims=True)
    ).astype(BF16)[None]
    if dwo.ndim == 3:
        dwo, dwo_gate = (
            half.reshape(S, R, B, C).transpose(1, 2, 0, 3).reshape(R, S * inner)
            for half in (dwo, dwo_gate)
        )
    raw = jnp.concatenate([dwo, dwo_gate], axis=1).astype(F32)
    in_weight_grad = raw * gain
    gain_grad = jnp.sum(raw * weight_rows, axis=1)
    conv_g, conv_b_g, dt_b_g, skip_g = misc[:taps], misc[taps], misc[taps + 1], misc[taps + 2]
    return (
        block_output, input_grad, states[:N][None], states[N:][None], gain_grad, in_weight_grad,
        conv_g, conv_b_g, xproj_g.T, dtproj_g, dt_b_g, decay_g, skip_g, out_weight_grad,
    )


def solution(mesh):
    both = ("batch", "seq")
    in_specs = (
        P("batch", "seq", None), P("batch", "seq", None), P("batch", None, None), P("batch", None),
        P(both), P(both, None), P(None, both), P(both), P(both, None), P(None, both), P(both),
        P(None, both), P(both), P(both, None),
    )
    out_specs = (
        P("batch", "seq", None), P("batch", "seq", None), P("batch", None, "seq"),
        P("batch", None, "seq"), P(both), P(both, None), P(None, both), P(both), P(both, None),
        P(None, both), P(both), P(None, both), P(both), P(both, None),
    )
    return jax.shard_map(
        functools.partial(body, mesh.shape["batch"], mesh.shape["seq"]),
        mesh=mesh, in_specs=in_specs, out_specs=out_specs, check_vma=False,
    )
```

```python
import functools

import jax
import jax.numpy as jnp
from jax import lax
from jax.experimental import pallas as pl
from jax.experimental.pallas import tpu as pltpu
from jax.sharding import PartitionSpec as P

GRAIN = 8
EPS = 1e-05
CORES = 2
F32 = jnp.float32
BF16 = jnp.bfloat16
MESH = pl.DeviceIdType.MESH
QUARTERS = 4
HALVES = 2
PARTS = 2
VMEM = pltpu.VMEM
ANY = pl.ANY
ROWS = 4
SMALLS = 4


def silu_slope(values):
    logistic = jax.nn.sigmoid(values)
    return logistic * (1.0 + values * (1.0 - logistic))


def enter(seq_count, batch_count, b, s):
    barrier = pltpu.get_barrier_semaphore()
    for i in range(1, seq_count):
        pl.semaphore_signal(
            barrier, inc=1, device_id=(b, lax.rem(s + i, seq_count)), device_id_type=MESH
        )
    for i in range(1, batch_count):
        pl.semaphore_signal(
            barrier, inc=1, device_id=(lax.rem(b + i, batch_count), s), device_id_type=MESH
        )
    pl.semaphore_wait(barrier, seq_count - 1 + batch_count - 1)


def remote(src, dst, send, recv, b, s):
    return pltpu.make_async_remote_copy(
        src_ref=src, dst_ref=dst, send_sem=send, recv_sem=recv, device_id=(b, s), device_id_type=MESH
    )


def strips(count, one, strip=16, first=0):
    def step(i, carry):
        one(pl.ds(pl.multiple_of(first + i * strip, strip), strip))
        return carry

    lax.fori_loop(0, count // strip, step, 0)


class LineGather:
    def __init__(self, S, b, s, src, out, sems):
        self.Z = S // CORES
        self.b, self.s, self.z, self.c = b, s, s // CORES, lax.rem(s, CORES)
        self.other = self.z * CORES + 1 - self.c
        self.src, self.out = src, out
        self.H = sems[0].shape[1]
        self.rows = src.shape[0] // self.H
        self.rs, self.rr, self.ls, self.lr, self.ss, self.sr = sems

    def piece(self, place, h):
        return self.out.at[place, pl.ds(h * self.rows, self.rows)]

    def own(self, h):
        return self.src.at[pl.ds(h * self.rows, self.rows)]

    def right(self, k, h):
        to = self.piece(self.s - CORES * k, h)
        return remote(
            self.own(h) if k == 0 else to, to, self.rs.at[k, h], self.rr.at[k, h], self.b, self.s + CORES
        )

    def left(self, k, h):
        to = self.piece(self.s + CORES * k, h)
        return remote(
            self.own(h) if k == 0 else to, to, self.ls.at[k, h], self.lr.at[k, h], self.b, self.s - CORES
        )

    def across(self, zz, h, mine=False):
        to = self.piece(zz * CORES + self.c, h)
        return remote(
            self.own(h) if mine else to, to, self.ss.at[zz, h], self.sr.at[zz, h], self.b, self.other
        )

    def arrived(self, place, h, sem):
        to = self.piece(place, h)
        remote(to, to, self.rs.at[0, h], sem, self.b, self.other).wait_recv()

    def start(self):
        for h in range(self.H):
            @pl.when(self.z + 1 < self.Z)
            def _():
                self.right(0, h).start()

            @pl.when(self.z > 0)
            def _():
                self.left(0, h).start()

            self.across(self.z, h, True).start()

    def relay(self, k, h):
        z, Z, s = self.z, self.Z, self.s

        @pl.when(z - k >= 0)
        def _():
            self.arrived(s - CORES * k, h, self.rr.at[k - 1, h])

            @pl.when(z + 1 < Z)
            def _():
                self.right(k, h).start()

            self.across(z - k, h).start()

        @pl.when(z + k < Z)
        def _():
            self.arrived(s + CORES * k, h, self.lr.at[k - 1, h])

            @pl.when(z > 0)
            def _():
                self.left(k, h).start()

            self.across(z + k, h).start()

    def drain(self):
        z, Z = self.z, self.Z
        for h in range(self.H):
            for k in range(Z):
                @pl.when((z - k >= 0) & (z + 1 < Z))
                def _():
                    self.right(k, h).wait_send()

                @pl.when((z + k < Z) & (z > 0))
                def _():
                    self.left(k, h).wait_send()

            for zz in range(Z):
                self.across(zz, h).wait_send()
                self.arrived(zz * CORES + 1 - self.c, h, self.sr.at[zz, h])


def line_gather_scratch(S, pieces):
    return [pltpu.SemaphoreType.DMA((S // CORES, pieces))] * 6


class LineSum:
    def __init__(self, S, b, s, src, acc, own, near, from_left, from_right, sems):
        self.Z = S // CORES
        self.b, self.z, self.c = b, s // CORES, lax.rem(s, CORES)
        self.s, self.sib = s, (s // CORES) * CORES + 1 - lax.rem(s, CORES)
        self.src, self.acc, self.own, self.near = src, acc, own, near
        self.from_left, self.from_right = from_left, from_right
        self.sib_s, self.sib_r, self.own_s, self.rs, self.rr, self.ls, self.lr = sems

    def sib_copy(self, zz):
        return remote(
            self.src.at[zz * CORES + 1 - self.c], self.near.at[zz], self.sib_s.at[zz],
            self.sib_r.at[zz], self.b, self.sib,
        )

    def own_copy(self, zz):
        return pltpu.make_async_copy(
            self.src.at[zz * CORES + self.c], self.own.at[zz], self.own_s.at[zz]
        )

    def half(self, h):
        rows = self.own.shape[1] // HALVES
        return pl.ds(h * rows, rows)

    def right(self, i, dest, h):
        at = self.half(h)
        return remote(
            self.own.at[dest, at], self.from_left.at[i, at], self.rs.at[i, h], self.rr.at[i, h],
            self.b, self.s + CORES,
        )

    def left(self, i, dest, h):
        at = self.half(h)
        return remote(
            self.own.at[dest, at], self.from_right.at[i, at], self.ls.at[i, h], self.lr.at[i, h],
            self.b, self.s - CORES,
        )

    def start(self):
        Z = self.Z

        def both(zz):
            self.sib_copy(zz).start()
            self.own_copy(zz).start()

        @pl.when(self.z == 0)
        def _():
            for j in range(Z):
                both(Z - 1 - j)

        @pl.when(self.z > 0)
        def _():
            for j in range(Z):
                both(j)

    def combine_one(self, zz):
        self.sib_copy(zz).wait_recv()
        self.own_copy(zz).wait()

        def one(at):
            total = self.own[zz, at].astype(F32) + self.near[zz, at].astype(F32)
            self.own[zz, at] = total.astype(BF16)

        strips(self.own.shape[1], one)

    def combine(self):
        Z = self.Z

        @pl.when(self.z == 0)
        def _():
            for j in range(Z):
                self.combine_one(Z - 1 - j)
                if j < Z - 1:
                    for h in range(HALVES):
                        self.right(j, Z - 1 - j, h).start()

        @pl.when(self.z > 0)
        def _():
            for j in range(Z):
                self.combine_one(j)
                if j < Z - 1:
                    @pl.when(self.z == Z - 1)
                    def _():
                        for h in range(HALVES):
                            self.left(j, j, h).start()

        def one(at):
            self.acc[at] = self.own[self.z, at].astype(F32)

        strips(self.own.shape[1], one)

    def take(self, buf, i, dest, last, h):
        rows = self.own.shape[1] // HALVES

        def one(at):
            if last:
                self.acc[at] = self.acc[at] + buf[i, at].astype(F32)
            else:
                total = self.own[dest, at].astype(F32) + buf[i, at].astype(F32)
                self.own[dest, at] = total.astype(BF16)

        strips(rows, one, 16, h * rows)

    def round(self, u, h):
        Z, z = self.Z, self.z

        @pl.when((z >= 1) & (z <= u))
        def _():
            i = u - z
            dest = Z - 1 - u + z
            self.right(i, dest, h).wait_recv()
            self.take(self.from_left, i, dest, u == Z - 1, h)
            if u < Z - 1:
                self.right(i, dest, h).start()

        @pl.when((z <= Z - 2) & (z >= Z - 1 - u))
        def _():
            i = u - (Z - 1) + z
            dest = u - (Z - 1) + z
            self.left(i, dest, h).wait_recv()
            self.take(self.from_right, i, dest, u == Z - 1, h)
            if u < Z - 1:
                self.left(i, dest, h).start()

    def drain(self):
        Z, z = self.Z, self.z
        for zz in range(Z):
            self.sib_copy(zz).wait_send()
        for i in range(Z - 1):
            @pl.when(i <= Z - 2 - z)
            def _():
                for h in range(HALVES):
                    self.right(i, Z - 1 - i, h).wait_send()

            @pl.when(i < z)
            def _():
                for h in range(HALVES):
                    self.left(i, i, h).wait_send()


def line_sum_scratch(S, rows, width):
    Z = S // CORES
    dma = pltpu.SemaphoreType.DMA
    return [
        VMEM((Z, rows, width), BF16), VMEM((Z, rows, width), BF16),
        VMEM((Z - 1, rows, width), BF16), VMEM((Z - 1, rows, width), BF16),
    ] + [dma((Z,))] * 3 + [dma((Z, HALVES))] * 4


class HomeSum:
    def __init__(self, B, S, b, s, src, out, buf, total, sems):
        self.B, self.S, self.b, self.s = B, S, b, s
        self.src, self.out, self.buf, self.total = src, out, buf, total
        self.s1, self.r1, self.s2, self.r2, self.loc = sems

    def first(self, j):
        bb = lax.rem(self.b + j, self.B)
        return remote(
            self.src.at[bb], self.buf.at[self.b], self.s1.at[j], self.r1.at[j], bb, self.s
        )

    def mine(self):
        return pltpu.make_async_copy(self.src.at[self.b], self.buf.at[self.b], self.loc.at[0])

    def lands(self):
        if self.out.ndim == 3:
            return [(slice(None), self.out.at[self.s])]
        B, S = self.B, self.S
        C = self.total.shape[2] // B
        return [
            (pl.ds(k * C, C), self.out.at[:, pl.ds(pl.multiple_of((k * S + self.s) * C, C), C)])
            for k in range(B)
        ]

    def second(self, i):
        ss = lax.rem(self.s + i, self.S)
        return [
            remote(
                self.total.at[ss, :, some], place, self.s2.at[i, k], self.r2.at[i, k], self.b, ss
            )
            for k, (some, place) in enumerate(self.lands())
        ]

    def start(self):
        for j in range(1, self.B):
            self.first(j).start()
        self.mine().start()

    def middle(self):
        self.mine().wait()
        for j in range(1, self.B):
            self.first(j).wait_recv()
        R = self.total.shape[1]

        def one(ss, carry):
            at = pl.ds(pl.multiple_of(ss * R, R), R)
            value = self.buf[0, at].astype(F32)
            for j in range(1, self.B):
                value = value + self.buf[j, at].astype(F32)
            self.total[ss] = value.astype(BF16)
            return carry

        lax.fori_loop(0, self.S, one, 0)
        for i in range(1, self.S):
            for copy in self.second(i):
                copy.start()
        for copy in self.kept():
            copy.start()

    def kept(self):
        return [
            pltpu.make_async_copy(self.total.at[self.s, :, some], place, self.loc.at[1 + k])
            for k, (some, place) in enumerate(self.lands())
        ]

    def drain(self):
        for copy in self.kept():
            copy.wait()
        for j in range(1, self.B):
            self.first(j).wait_send()
        for i in range(1, self.S):
            for copy in self.second(i):
                copy.wait()


def home_sum_scratch(B, S, shape):
    rows, width = shape
    dma = pltpu.SemaphoreType.DMA
    return [
        VMEM((B, rows, width), BF16), VMEM((S, rows // S, width), BF16),
        dma((B,)), dma((B,)), dma((S, B)), dma((S, B)), dma((1 + B,)),
    ]


def home_sum_shape(B, S, shape):
    rows, width = shape
    if (width // B) % 128 == 0:
        return jax.ShapeDtypeStruct((rows // S, S * width), BF16)
    return jax.ShapeDtypeStruct((S, rows // S, width), BF16)


def gather_kernel(
    B, S, made, x_ref, w_ref, g_ref, *refs
):
    smalls, refs = refs[: SMALLS - 1], refs[SMALLS - 1 :]
    rows, refs = refs[:ROWS], refs[ROWS:]
    xg_ref, wf_ref, refs = refs[0], refs[1], refs[2:]
    smalls_out, refs = refs[:SMALLS], refs[SMALLS:]
    xh_ref, wp_ref, tail_ref, w1s, w1r, w2s, w2r, ps, pr, loc, *line_sems = refs
    Z = S // CORES
    b = lax.axis_index("batch")
    s = lax.axis_index("seq")
    line = LineGather(S, b, s, xh_ref, xg_ref, line_sems)
    values = [row[...].astype(F32) for row in rows]
    free = tail_ref.shape[0] - sum(value.shape[0] for value in values)
    values.append(jnp.zeros((free, tail_ref.shape[1]), F32))
    tail_ref[...] = jnp.concatenate(values, axis=0).astype(BF16)
    smalls = smalls + (tail_ref,)
    if made:
        R, C = w_ref.shape[0], w_ref.shape[1] // (2 * B * S)

        def one(at):
            rows = w_ref[at].astype(F32) * g_ref[at]
            for place in range(2 * B):
                for to in range(S):
                    first = (place * S + to) * C
                    wp_ref[to, at, place * C : place * C + C] = rows[:, first : first + C].astype(BF16)

        strips(R, one)
        w_ref = wp_ref
    enter(S, B, b, s)

    def batch_copy(i, j):
        src_s = lax.rem(s + S - i, S)
        src = w_ref.at[s] if i == 0 else wf_ref.at[b, src_s]
        return remote(
            src, wf_ref.at[b, src_s], w2s.at[j - 1, i], w2r.at[j - 1, i], lax.rem(b + j, B), s
        )

    def seq_copy(i):
        dst_s = lax.rem(s + i, S)
        return remote(w_ref.at[dst_s], wf_ref.at[b, s], w1s.at[i], w1r.at[i], b, dst_s)

    def small_copy(n, j):
        return remote(
            smalls[n], smalls_out[n].at[b], ps.at[n, j - 1], pr.at[n, j - 1], lax.rem(b + j, B), s
        )

    for i in range(1, S):
        seq_copy(i).start()
    for j in range(1, B):
        for n in range(SMALLS):
            small_copy(n, j).start()
    for j in range(1, B):
        batch_copy(0, j).start()

    def norm(at):
        x = x_ref[at].astype(F32)
        xh_ref[at] = (x * lax.rsqrt(jnp.mean(x * x, axis=-1, keepdims=True) + EPS)).astype(BF16)

    strips(x_ref.shape[0], norm)

    line.start()
    locals_ = [
        pltpu.make_async_copy(xh_ref, xg_ref.at[s], loc.at[0]),
        pltpu.make_async_copy(w_ref.at[s], wf_ref.at[b, s], loc.at[1]),
    ] + [
        pltpu.make_async_copy(smalls[n], smalls_out[n].at[b], loc.at[2 + n]) for n in range(SMALLS)
    ]
    for copy in locals_:
        copy.start()

    for i in range(1, S):
        seq_copy(i).wait_recv()
        for j in range(1, B):
            batch_copy(i, j).start()

    for k in range(1, Z):
        for h in range(QUARTERS):
            line.relay(k, h)

    line.drain()
    for i in range(1, S):
        seq_copy(i).wait_send()
    for i in range(S):
        src_s = lax.rem(s + S - i, S)
        for j in range(1, B):
            src_b = lax.rem(b + B - j, B)
            batch_copy(i, j).wait_send()
            remote(
                wf_ref.at[src_b, src_s], wf_ref.at[src_b, src_s],
                w2s.at[j - 1, i], w2r.at[j - 1, i], src_b, s,
            ).wait_recv()
    for j in range(1, B):
        src_b = lax.rem(b + B - j, B)
        for n in range(SMALLS):
            small_copy(n, j).wait_send()
            place = smalls_out[n].at[src_b]
            remote(place, place, ps.at[n, j - 1], pr.at[n, j - 1], src_b, s).wait_recv()
    for copy in locals_:
        copy.wait()


def gather_all(B, S, x, weight, gain, smalls, rows):
    Z = S // CORES
    R, E = weight.shape
    C = E // (2 * B * S)
    made = C % 128 == 0 and R % 16 == 0
    if not made:
        weight = (weight.astype(F32) * gain).astype(BF16).reshape(R, 2 * B, S, C)
        weight = weight.transpose(2, 0, 1, 3).reshape(S, R, E // S)
    dma = pltpu.SemaphoreType.DMA
    return pl.pallas_call(
        functools.partial(gather_kernel, B, S, made),
        out_shape=(
            jax.ShapeDtypeStruct((S,) + x.shape, BF16),
            jax.ShapeDtypeStruct((B, S, R, E // S), BF16),
        ) + tuple(jax.ShapeDtypeStruct((B,) + small.shape, BF16) for small in smalls)
        + (jax.ShapeDtypeStruct((B, 16, rows[0].shape[1]), BF16),),
        in_specs=[pl.BlockSpec(memory_space=VMEM)] * (2 + SMALLS + ROWS),
        out_specs=(pl.BlockSpec(memory_space=ANY),) * (2 + SMALLS),
        scratch_shapes=[
            VMEM(x.shape, BF16), VMEM((S, R, E // S), BF16), VMEM((16, rows[0].shape[1]), BF16),
            dma((S,)), dma((S,)), dma((B - 1, S)), dma((B - 1, S)),
            dma((SMALLS, B - 1)), dma((SMALLS, B - 1)), dma((2 + SMALLS,)),
        ]
        + line_gather_scratch(S, QUARTERS),
        compiler_params=pltpu.CompilerParams(collective_id=1, has_side_effects=True),
        name="gather_all",
    )(x, weight, gain, *smalls, *rows)


def token_sums(parts):
    width = parts[0].shape[1]
    row = lax.broadcasted_iota(jnp.int32, (8, width), 0)
    for bit in (1, 2, 4):
        low = (row & bit) == 0
        merged = []
        for k in range(0, len(parts), 2):
            first, second = parts[k], parts[k + 1]
            merged.append(
                jnp.where(low, first, second) + pltpu.roll(jnp.where(low, second, first), bit, 0)
            )
        parts = merged
    return parts[0]


def forward_kernel(
    B, S, groups, N, keep_ref, part_ref, act_ref, dtproj_ref, bias_ref, rate_ref, init_ref, cot_ref,
    ow_ref,
    read_ref, hs_ref, last_ref, step_out, pre_out, rank_out, coef_out, cots_ref, ows_ref,
    h_ref, act_f32, terms, ranks, coefs, p_s, p_r, rank_s, rank_r, coef_s, coef_r,
    ow_s, ow_r, loc, *line_sems,
):
    rank = ranks.shape[1]
    block = pl.program_id(0)
    width = groups * GRAIN
    Z = S // CORES
    b = lax.axis_index("batch")
    s = lax.axis_index("seq")
    line = LineGather(S, b, s, cot_ref, cots_ref, line_sems)

    def ow_copy(j):
        return remote(ow_ref, ows_ref.at[b], ow_s.at[j], ow_r.at[j], lax.rem(b + j, B), s)

    def mine():
        return [
            pltpu.make_async_copy(cot_ref, cots_ref.at[s], loc.at[0]),
            pltpu.make_async_copy(ow_ref, ows_ref.at[b], loc.at[1]),
        ]

    def term_copy(i):
        return remote(part_ref.at[i], terms.at[s], p_s.at[i], p_r.at[s], b, i)

    def sum_copies(to, source):
        return [
            remote(ranks.at[source], ranks.at[source], rank_s.at[to], rank_r.at[source], b, to),
            remote(coefs.at[source], coefs.at[source], coef_s.at[to], coef_r.at[source], b, to),
        ]

    @pl.when(block == 0)
    def _():
        h_ref[...] = init_ref[...]
        enter(S, B, b, s)
        for i in range(S):
            @pl.when(s != i)
            def _():
                term_copy(i).start()

        total = part_ref[s].astype(F32)
        for i in range(1, S):
            source = lax.rem(s + i, S)
            remote(part_ref.at[s], terms.at[source], p_s.at[0], p_r.at[source], b, source).wait_recv()
            total = total + terms[source].astype(F32)
        ranks[s] = total[:rank].astype(BF16)
        coefs[s] = total[rank:]
        for i in range(S):
            @pl.when(s != i)
            def _():
                for copy in sum_copies(i, s):
                    copy.start()

        line.start()
        for j in range(1, B):
            ow_copy(j).start()
        for copy in mine():
            copy.start()

    for k in range(1, Z):
        for h in range(HALVES):
            if HALVES * k + h < S - 1:
                @pl.when(block == HALVES * k + h)
                def _():
                    line.relay(k, h)

    @pl.when(s != block)
    def _():
        for copy in sum_copies(block, block):
            copy.wait_recv()

    here = ranks[block]
    coef_here = coefs[block]
    rank_out[0] = here
    coef_out[0] = coef_here
    pre = lax.dot_general(here, dtproj_ref[...], (((0,), (0,)), ((), ())), preferred_element_type=F32)
    pre = pre + bias_ref[...]
    pre_out[0] = pre
    step_out[0] = jnp.maximum(pre, 0.0) + jnp.log1p(jnp.exp(-jnp.abs(pre)))
    act_f32[...] = act_ref[0].astype(F32)
    rate = rate_ref[...]

    def group(g, h):
        at = pl.multiple_of(g * GRAIN, GRAIN)
        coef = pltpu.roll(coef_here, lax.rem(width - at, width), 1)
        step = step_out[0, pl.ds(at, GRAIN), :]
        drive = step * act_f32[pl.ds(at, GRAIN), :]
        h = h * keep_ref[block * groups + g]
        parts = []
        for j in range(GRAIN):
            decay = jnp.exp(step[j : j + 1] * rate)
            h = decay * h + coef[:N, j : j + 1] * drive[j : j + 1]
            hs_ref[0, at + j] = h
            seen = coef[N:, j : j + 1] * h
            parts.append(seen[:8] + seen[8:])
        read_ref[0, pl.ds(at, GRAIN), :] = token_sums(parts)
        return h

    h = lax.fori_loop(0, groups, group, h_ref[...])
    h_ref[...] = h
    last_ref[...] = h

    @pl.when(block == S - 1)
    def _():
        for k in range(1, Z):
            for h in range(HALVES):
                if HALVES * k + h >= S - 1:
                    line.relay(k, h)
        for i in range(S):
            @pl.when(s != i)
            def _():
                term_copy(i).wait_send()
                for copy in sum_copies(i, s):
                    copy.wait_send()

        line.drain()
        for j in range(1, B):
            source = lax.rem(b + B - j, B)
            ow_copy(j).wait_send()
            remote(ows_ref.at[source], ows_ref.at[source], ow_s.at[j], ow_r.at[j], source, s).wait_recv()
        for copy in mine():
            copy.wait()


def scan_forward(B, keep, part, act, dtproj, bias, rate, init, cot, ow):
    S, width, inner = act.shape
    N = rate.shape[0]
    rank = dtproj.shape[0]
    groups = width // GRAIN
    Z = S // CORES
    token = pl.BlockSpec((1, width, inner), lambda i: (i, 0, 0))
    whole = pl.BlockSpec(memory_space=VMEM)
    hbm = pl.BlockSpec(memory_space=ANY)
    state = pl.BlockSpec((N, inner), lambda i: (0, 0))
    dma = pltpu.SemaphoreType.DMA
    tokens = jax.ShapeDtypeStruct((S, width, inner), F32)
    return pl.pallas_call(
        functools.partial(forward_kernel, B, S, groups, N),
        grid=(S,),
        out_shape=(
            tokens,
            jax.ShapeDtypeStruct((S, width, N, inner), F32),
            jax.ShapeDtypeStruct((N, inner), F32),
            tokens,
            tokens,
            jax.ShapeDtypeStruct((S, rank, width), BF16),
            jax.ShapeDtypeStruct((S, 2 * N, width), F32),
            jax.ShapeDtypeStruct((S,) + cot.shape, BF16),
            jax.ShapeDtypeStruct((B,) + ow.shape, BF16),
        ),
        in_specs=[
            pl.BlockSpec(memory_space=pltpu.SMEM), whole, token, whole, whole, state, state, whole, whole,
        ],
        out_specs=(
            token, pl.BlockSpec((1, width, N, inner), lambda i: (i, 0, 0, 0)), state, token, token,
            pl.BlockSpec((1, rank, width), lambda i: (i, 0, 0)),
            pl.BlockSpec((1, 2 * N, width), lambda i: (i, 0, 0)),
            hbm, hbm,
        ),
        scratch_shapes=[
            VMEM((N, inner), F32), VMEM((width, inner), F32), VMEM(part.shape, BF16),
            VMEM((S, rank, width), BF16), VMEM((S, 2 * N, width), F32),
            dma((S,)), dma((S,)), dma((S,)), dma((S,)), dma((S,)), dma((S,)),
            dma((B,)), dma((B,)), dma((2,)),
        ]
        + line_gather_scratch(S, HALVES),
        compiler_params=pltpu.CompilerParams(collective_id=5, has_side_effects=True),
        name="scan_forward",
    )(keep, part, act, dtproj, bias, rate, init, cot, ow)


def backward_kernel(
    B, S, groups, N, keep_ref, step_ref, pre_ref, act_ref, pull_ref, coef_ref, hs_ref, before_ref,
    rate_ref, init_ref, dtproj_ref, op_ref, dg_ref, og_ref,
    step_low_ref, act_grad_ref, decay_ref, start_ref, bias_ref, bo_ref, dgo_ref, ogs_ref, proj_ref,
    g_ref, prior_ref, act_f32, step_grad, sends, near, mid, terms, fin,
    a_s, a_r, t_s, t_r, f_s, f_r, own, og_s, og_r, og_own, *scratch,
):
    turn = pl.program_id(0)
    block = pl.num_programs(0) - 1 - turn
    width = groups * GRAIN
    b = lax.axis_index("batch")
    s = lax.axis_index("seq")
    line = LineSum(S, b, s, op_ref, bo_ref, *scratch[:4], scratch[4:11])
    home = HomeSum(B, S, b, s, dg_ref, dgo_ref, *scratch[11:13], scratch[13:])

    def og_copy(j):
        bb = lax.rem(b + j, B)
        return remote(og_ref.at[bb], ogs_ref.at[b], og_s.at[j], og_r.at[j], bb, s)

    def og_keep():
        return pltpu.make_async_copy(og_ref.at[b], ogs_ref.at[b], og_own.at[0])

    Z = S // CORES
    z = s // CORES
    c = lax.rem(s, CORES)
    sib = z * CORES + 1 - c

    def half_copy(i):
        return remote(sends.at[i, 1 - c], near.at[i], a_s.at[i], a_r.at[i], b, sib)

    def chip_copy(i, k):
        to = lax.rem(z + k, Z)
        return remote(
            mid.at[i], terms.at[i, z], t_s.at[k, i], t_r.at[k, i], b, to * CORES + c
        )

    def final_copy(i):
        return remote(fin.at[i], proj_ref.at[i, c], f_s.at[i], f_r.at[i], b, sib)

    def final_keep(i):
        return pltpu.make_async_copy(fin.at[i], proj_ref.at[i, c], own.at[i])

    def over_cores(i):
        half_copy(i).wait_recv()
        mid[i] = (sends[i, c].astype(F32) + near[i].astype(F32)).astype(BF16)
        for k in range(1, Z):
            chip_copy(i, k).start()

    def over_chips(i):
        value = mid[i].astype(F32)
        for k in range(1, Z):
            chip_copy(i, k).wait_recv()
            value = value + terms[i, lax.rem(z + Z - k, Z)].astype(F32)
        fin[i] = value.astype(BF16)
        final_copy(i).start()
        final_keep(i).start()

    @pl.when(turn == 0)
    def _():
        g_ref[...] = jnp.zeros_like(g_ref)
        decay_ref[...] = jnp.zeros_like(decay_ref)
        bias_ref[...] = jnp.zeros_like(bias_ref)
        enter(S, B, b, s)
        line.start()
        home.start()
        for j in range(1, B):
            og_copy(j).start()
        og_keep().start()

    @pl.when(turn == 1)
    def _():
        line.combine()

    for u in range(1, S // CORES):
        for h in range(HALVES):
            @pl.when(turn == HALVES * u + h)
            def _():
                line.round(u, h)

    @pl.when(turn == S - 3)
    def _():
        home.middle()

    @pl.when(turn >= 2)
    def _():
        over_cores(S + 1 - turn)


    act_f32[...] = act_ref[0].astype(F32)

    prior_ref[...] = jnp.where(block > 0, before_ref[0, 0], init_ref[...])
    inner = step_ref.shape[2]
    lane = lax.broadcasted_iota(jnp.int32, (2 * N, width), 1)

    parts = PARTS if inner % (PARTS * 128) == 0 else 1
    lanes = [pl.ds(i * (inner // parts), inner // parts) for i in range(parts)]

    def fold(value):
        count = value.shape[1] // 128
        return sum((value[:, i * 128 : (i + 1) * 128] for i in range(1, count)), value[:, :128])

    def group(k, carry):
        states, coef_grad = carry
        g = groups - 1 - k
        at = pl.multiple_of(g * GRAIN, GRAIN)
        coef = pltpu.roll(coef_ref[0], lax.rem(width - at, width), 1)
        keep = keep_ref[block * groups + g]
        after = []
        entries = [0.0] * GRAIN
        leaves = [0.0] * GRAIN
        for (carried, total), some in zip(states, lanes):
            step = step_ref[0, pl.ds(at, GRAIN), some]
            act = act_f32[pl.ds(at, GRAIN), some]
            pull = pull_ref[0, pl.ds(at, GRAIN), some]
            rate = rate_ref[:, some]
            drive = step * act
            rate_parts = [None] * GRAIN
            drive_parts = [None] * GRAIN
            for j in reversed(range(GRAIN)):
                step_j = step[j : j + 1]
                decay = jnp.exp(step_j * rate)
                costate = coef[N:, j : j + 1] * pull[j : j + 1] + carried
                carried = decay * costate
                if j == 0:
                    prior = jnp.where(
                        g > 0, hs_ref[0, jnp.maximum(at - 1, 0), :, some], prior_ref[:, some]
                    ) * keep
                else:
                    prior = hs_ref[0, at + j - 1, :, some]
                rate_grad = carried * prior
                if j == 0:
                    carried = carried * keep
                total = total + rate_grad * step_j
                part = rate_grad * rate
                rate_parts[j] = part[:8] + part[8:]
                part = costate * coef[:N, j : j + 1]
                drive_parts[j] = part[:8] + part[8:]
                entries[j] = entries[j] + fold(costate * drive[j : j + 1])
                leaves[j] = leaves[j] + fold(hs_ref[0, at + j, :, some] * pull[j : j + 1])
            drive_pull = token_sums(drive_parts)
            step_grad[pl.ds(at, GRAIN), some] = token_sums(rate_parts) + drive_pull * act
            act_grad_ref[0, pl.ds(at, GRAIN), some] = drive_pull * step
            after.append((carried, total))
        for j in range(GRAIN):
            both = jnp.sum(jnp.concatenate([entries[j], leaves[j]], axis=0), axis=1, keepdims=True)
            coef_grad = jnp.where(lane == at + j, both, coef_grad)
        return tuple(after), coef_grad

    states, coef_grad = lax.fori_loop(
        0, groups, group,
        (
            tuple((g_ref[:, some], decay_ref[:, some]) for some in lanes),
            jnp.zeros((2 * N, width), F32),
        ),
    )
    carried = jnp.concatenate([state[0] for state in states], axis=1)
    total = jnp.concatenate([state[1] for state in states], axis=1)
    g_ref[...] = carried
    start_ref[...] = carried
    decay_ref[...] = total
    pre_grad = step_grad[...] * jax.nn.sigmoid(pre_ref[0])
    bias_ref[...] = bias_ref[...] + jnp.sum(pre_grad, axis=0, keepdims=True)
    low = pre_grad.astype(BF16)
    step_low_ref[0] = low
    rank_grad = lax.dot_general(
        dtproj_ref[...], low, (((1,), (1,)), ((), ())), preferred_element_type=F32
    )
    low = jnp.concatenate([rank_grad, coef_grad], axis=0).astype(BF16)
    rows = sends.shape[2]
    for half in range(CORES):
        sends[block, half] = low[half * rows : (half + 1) * rows]
    half_copy(block).start()

    @pl.when(turn == S - 1)
    def _():
        over_cores(1)
        over_cores(0)
        line.drain()
        home.drain()
        for i in reversed(range(S)):
            over_chips(i)
        for i in range(S):
            half_copy(i).wait_send()
            for k in range(1, Z):
                chip_copy(i, k).wait_send()
            final_copy(i).wait_send()
            remote(fin.at[i], proj_ref.at[i, 1 - c], f_s.at[i], f_r.at[i], b, sib).wait_recv()
            final_keep(i).wait()
        og_keep().wait()
        for j in range(1, B):
            source = lax.rem(b + B - j, B)
            og_copy(j).wait_send()
            remote(ogs_ref.at[source], ogs_ref.at[source], og_s.at[j], og_r.at[j], source, s).wait_recv()


def scan_backward(B, keep, step, pre, act, pull, coef, hs, rate, init, dtproj, op, dg, og):
    S, width, inner = step.shape
    N = rate.shape[0]
    rank = dtproj.shape[0]
    groups = width // GRAIN
    token = pl.BlockSpec((1, width, inner), lambda i: (S - 1 - i, 0, 0))
    coefs = pl.BlockSpec((1, 2 * N, width), lambda i: (S - 1 - i, 0, 0))
    state = pl.BlockSpec((N, inner), lambda i: (0, 0))
    whole = pl.BlockSpec(memory_space=VMEM)
    hbm = pl.BlockSpec(memory_space=ANY)
    dma = pltpu.SemaphoreType.DMA
    half = ((rank + 2 * N) // CORES, width)
    Z = S // CORES
    return pl.pallas_call(
        functools.partial(backward_kernel, B, S, groups, N),
        grid=(S,),
        out_shape=(
            jax.ShapeDtypeStruct((S, width, inner), BF16),
            jax.ShapeDtypeStruct((S, width, inner), F32),
            jax.ShapeDtypeStruct((N, inner), F32),
            jax.ShapeDtypeStruct((N, inner), F32),
            jax.ShapeDtypeStruct((1, inner), F32),
            jax.ShapeDtypeStruct(op.shape[1:], F32),
            home_sum_shape(B, S, dg.shape[1:]),
            jax.ShapeDtypeStruct(og.shape, BF16),
            jax.ShapeDtypeStruct((S, CORES) + half, BF16),
        ),
        in_specs=[
            pl.BlockSpec(memory_space=pltpu.SMEM), token, token, token, token, coefs,
            pl.BlockSpec((1, width, N, inner), lambda i: (S - 1 - i, 0, 0, 0)),
            pl.BlockSpec(
                (1, 1, N, inner), lambda i: (jnp.maximum(S - 2 - i, 0), width - 1, 0, 0)
            ),
            state, state, whole, hbm, hbm, hbm,
        ],
        out_specs=(
            token, token, state, state, pl.BlockSpec((1, inner), lambda i: (0, 0)), whole, hbm, hbm, hbm,
        ),
        scratch_shapes=[
            VMEM((N, inner), F32), VMEM((N, inner), F32), VMEM((width, inner), F32),
            VMEM((width, inner), F32), VMEM((S, CORES) + half, BF16), VMEM((S,) + half, BF16),
            VMEM((S,) + half, BF16), VMEM((S, Z) + half, BF16), VMEM((S,) + half, BF16),
            dma((S,)), dma((S,)), dma((Z, S)), dma((Z, S)), dma((S,)), dma((S,)), dma((S,)),
            dma((B,)), dma((B,)), dma((1,)),
        ]
        + line_sum_scratch(S, *op.shape[1:])
        + home_sum_scratch(B, S, dg.shape[1:]),
        compiler_params=pltpu.CompilerParams(collective_id=6, has_side_effects=True),
        name="scan_backward",
    )(keep, step, pre, act, pull, coef, hs, hs, rate, init, dtproj, op, dg, og)


def columns(ref, i, width):
    if ref.ndim == 3:
        return ref.at[i]
    return ref.at[:, pl.ds(pl.multiple_of(i * width, width), width)]


def scatter_kernel(B, S, count, C, dx_ref, dw_ref, st_ref, *refs):
    grads, refs = refs[:count], refs[count:]
    dxo_ref, dwo_ref, sto_ref, refs = refs[0], refs[1], refs[2], refs[3:]
    sums, refs = refs[:count], refs[count:]
    bufs, refs = refs[:count], refs[count:]
    g_s, g_r, st_s, st_r, loc, *scratch = refs
    b = lax.axis_index("batch")
    s = lax.axis_index("seq")
    line = LineSum(S, b, s, dx_ref, dxo_ref, *scratch[:4], scratch[4:11])
    home = HomeSum(B, S, b, s, dw_ref, dwo_ref, *scratch[11:13], scratch[13:])
    enter(S, B, b, s)

    def grad_copy(n, j):
        bb = lax.rem(b + j, B)
        return remote(
            columns(grads[n], bb, C), bufs[n].at[b], g_s.at[n, j], g_r.at[n, j], bb, s
        )

    def grad_here(n):
        return pltpu.make_async_copy(columns(grads[n], b, C), bufs[n].at[b], loc.at[n])

    def st_place(j):
        place = j * S + s
        return place // B, lax.rem(place, B)

    def st_copy(j):
        to, slot = st_place(j)
        return remote(
            columns(st_ref, j, C), columns(sto_ref, slot, C), st_s.at[j], st_r.at[slot], b, to
        )

    def st_local(j):
        to, slot = st_place(j)
        return pltpu.make_async_copy(columns(st_ref, j, C), columns(sto_ref, slot, C), st_s.at[j])

    line.start()
    home.start()
    for n in range(count):
        for j in range(1, B):
            grad_copy(n, j).start()
        grad_here(n).start()
    for j in range(B):
        to, slot = st_place(j)

        @pl.when(to != s)
        def _():
            st_copy(j).start()

        @pl.when(to == s)
        def _():
            st_local(j).start()

    Z = S // CORES
    line.combine()
    for u in range(1, Z):
        for h in range(HALVES):
            line.round(u, h)
        if u == max(Z - 2, 1):
            home.middle()
    for n in range(count):
        grad_here(n).wait()
        for j in range(1, B):
            source = lax.rem(b + B - j, B)
            place = bufs[n].at[source]
            remote(place, place, g_s.at[n, j], g_r.at[n, j], source, s).wait_recv()
        total = bufs[n][0]
        for j in range(1, B):
            total = total + bufs[n][j]
        sums[n][...] = total

    line.drain()
    home.drain()
    for n in range(count):
        for j in range(1, B):
            grad_copy(n, j).wait_send()
    for j in range(B):
        to, slot = st_place(j)

        @pl.when(to != s)
        def _():
            st_copy(j).wait_send()

        @pl.when(to == s)
        def _():
            st_local(j).wait()

    for slot in range(B):
        source = lax.rem(s * B + slot, S)

        @pl.when(source != s)
        def _():
            place = columns(sto_ref, slot, C)
            remote(place, place, st_s.at[0], st_r.at[slot], b, source).wait_recv()


def scatter_all(B, S, dx, dw, st, grads):
    _, rows, D = dx.shape
    inner = dw.shape[2]
    C = inner // B
    if C % 128:

        def parts(value):
            return value.reshape(value.shape[0], B, C).transpose(1, 0, 2)

        st, grads = parts(st), [parts(grad) for grad in grads]
    dma = pltpu.SemaphoreType.DMA
    count = len(grads)
    heights = [grad.shape[-2] for grad in grads]
    return pl.pallas_call(
        functools.partial(scatter_kernel, B, S, count, C),
        out_shape=(
            jax.ShapeDtypeStruct((rows, D), F32),
            home_sum_shape(B, S, dw.shape[1:]),
            jax.ShapeDtypeStruct(st.shape, F32),
        ) + tuple(jax.ShapeDtypeStruct((height, C), F32) for height in heights),
        in_specs=[pl.BlockSpec(memory_space=ANY)] * (3 + count),
        out_specs=(pl.BlockSpec(memory_space=VMEM),) * (3 + count),
        scratch_shapes=[VMEM((B, height, C), F32) for height in heights]
        + [dma((count, B)), dma((count, B)), dma((B,)), dma((B,)), dma((count,))]
        + line_sum_scratch(S, rows, D)
        + home_sum_scratch(B, S, dw.shape[1:]),
        compiler_params=pltpu.CompilerParams(collective_id=4, has_side_effects=True),
        name="scatter_all",
    )(dx, dw, st, *grads)


def body(
    B, S,
    block_input, cotangent, init_state, doc_starts, norm_gain, in_weight, conv_weight, conv_bias,
    xproj_weight, dtproj_weight, dt_bias, decay_log, skip_gain, out_weight,
):
    _, width, D = block_input.shape
    T = S * width
    R = in_weight.shape[0]
    C = conv_bias.shape[0]
    inner = B * C
    taps = conv_weight.shape[0]
    rank = dtproj_weight.shape[0]
    N = decay_log.shape[0]
    s = lax.axis_index("seq")

    x = block_input[0].astype(F32)
    inv_rms = lax.rsqrt(jnp.mean(x * x, axis=-1, keepdims=True) + EPS)
    xhat = (x * inv_rms).astype(BF16)
    gain = norm_gain.astype(F32)[:, None]
    weight_rows = in_weight.astype(F32)
    rows = [
        dtproj_weight, xproj_weight.T, decay_log, conv_weight,
        conv_bias[None], dt_bias[None], skip_gain[None],
    ]
    xg, wf, *smalls = gather_all(B, S, block_input[0], in_weight, gain, rows[:3], rows[3:])
    tokens = xg.reshape(T, D)
    full_in = wf.reshape(D, 2 * inner)
    dtproj, xproj_t, decay_full, tail = (
        small.transpose(1, 0, 2).reshape(small.shape[1], inner) for small in smalls
    )
    conv_full, conv_b, dt_b, skip = (
        tail[:taps], tail[taps : taps + 1], tail[taps + 1 : taps + 2], tail[taps + 2 : taps + 3]
    )
    conv_full = conv_full.astype(F32)
    skip = skip.astype(F32)

    places = jnp.arange(T, dtype=jnp.int32)
    starts = doc_starts[0]

    def doc_number(at):
        return jnp.sum((at[:, None] >= starts[None, :]).astype(jnp.int32), axis=1)

    doc_here = doc_number(places)
    masks = [
        (doc_number(places - (taps - 1 - tap)) == doc_here).astype(F32)[:, None]
        for tap in range(taps)
    ]
    heads = GRAIN * jnp.arange(T // GRAIN, dtype=jnp.int32)
    keep = 1.0 - jnp.any(heads[:, None] == starts[None, :], axis=1).astype(F32)

    mixed = jnp.dot(tokens, full_in, preferred_element_type=F32)
    conv_in = mixed[:, :inner].astype(BF16)
    gate_pre = mixed[:, inner:]
    extended = jnp.pad(conv_in, ((taps - 1, 0), (0, 0))).astype(F32)
    conv_out = jnp.zeros((T, inner), F32) + conv_b.astype(F32)
    for tap in range(taps):
        conv_out = conv_out + conv_full[tap] * extended[tap : tap + T] * masks[tap]
    act_in = jax.nn.silu(conv_out).astype(BF16)
    act = act_in.astype(F32)

    part = lax.dot_general(xproj_t, act_in, (((1,), (1,)), ((), ())), preferred_element_type=F32)
    part = part.astype(BF16).reshape(-1, S, width).transpose(1, 0, 2)
    rate = -jnp.exp(decay_full.astype(F32))
    start = init_state[0].reshape(N, B, S, C)
    start = lax.dynamic_index_in_dim(start, s, 2, False).reshape(N, inner)
    act3 = act_in.reshape(S, width, inner)
    readout, hs, last, step, step_pre, rank_in, coef, cot, full_out = scan_forward(
        B, keep, part, act3, dtproj, dt_b.astype(F32), rate, start, cotangent[0], out_weight
    )
    cot = cot.reshape(T, D)
    full_out = full_out.reshape(inner, D)

    mixed_out = readout.reshape(T, inner) + skip * act
    gate_act = jax.nn.silu(gate_pre)
    gated_out = (mixed_out * gate_act).astype(BF16)
    out_part = jnp.dot(gated_out, full_out, preferred_element_type=F32)
    out_part = out_part.astype(BF16).reshape(S, width, D)

    gated_grad = lax.dot_general(cot, full_out, (((1,), (1,)), ((), ())), preferred_element_type=F32)
    mixer_grad = gated_grad * gate_act
    gate_low = (gated_grad * mixed_out * silu_slope(gate_pre)).astype(BF16)
    skip_grad = jnp.sum(mixer_grad * act, axis=0)
    out_grad_part = lax.dot_general(
        gated_out, cot, (((0,), (0,)), ((), ())), preferred_element_type=F32
    )
    out_grad_part = out_grad_part.astype(BF16).reshape(B, C, D)
    dw_gate = lax.dot_general(tokens, gate_low, (((0,), (0,)), ((), ())), preferred_element_type=F32)
    dw_gate = dw_gate.astype(BF16).reshape(B, S * R, inner)

    step_low, act_grad, decay_grad, start_grad, dt_bias_grad, out_sum, dwo_gate, terms, proj_grad = (
        scan_backward(
            B, keep, step, step_pre, act3, mixer_grad.reshape(S, width, inner), coef, hs, rate, start,
            dtproj, out_part, dw_gate, out_grad_part,
        )
    )
    proj_grad = proj_grad.reshape(S, rank + 2 * N, width)
    block_output = (x + out_sum).astype(BF16)[None]
    out_weight_grad = jnp.sum(terms.astype(F32), axis=0)
    decay_log_grad = decay_grad * rate
    dtproj_grad = jnp.einsum("skt,std->kd", rank_in, step_low, preferred_element_type=F32)
    xproj_grad = jnp.einsum(
        "set,std->ed", proj_grad, act3, preferred_element_type=F32
    )
    act_total = (
        act_grad.reshape(T, inner)
        + mixer_grad * skip
        + jnp.einsum("set,ed->std", proj_grad, xproj_t, preferred_element_type=F32).reshape(T, inner)
    )
    conv_grad = act_total * silu_slope(conv_out)
    conv_bias_grad = jnp.sum(conv_grad, axis=0)
    tap_grads = []
    conv_in_grad = jnp.zeros((T, inner), F32)
    for tap in range(taps):
        masked = conv_grad * masks[tap]
        tap_grads.append(jnp.sum(masked * extended[tap : tap + T], axis=0))
        back = taps - 1 - tap
        conv_in_grad = conv_in_grad + jnp.pad(conv_full[tap] * masked, ((0, back), (0, 0)))[back:]
    conv_low = conv_in_grad.astype(BF16)
    mixed_grad = jnp.concatenate([conv_low, gate_low], axis=-1)

    dw = lax.dot_general(tokens, conv_low, (((0,), (0,)), ((), ())), preferred_element_type=F32)
    dw = dw.astype(BF16).reshape(B, S * R, inner)
    dx = lax.dot_general(mixed_grad, full_in, (((1,), (1,)), ((), ())), preferred_element_type=F32)
    dx = dx.astype(BF16).reshape(S, width, D)
    misc = jnp.concatenate(
        [jnp.stack(tap_grads), conv_bias_grad[None], dt_bias_grad, skip_grad[None]]
        + [jnp.zeros((-(taps + 3) % 8, inner), F32)],
        axis=0,
    )
    gained, dwo, states, dtproj_g, xproj_g, decay_g, misc = scatter_all(
        B, S, dx, dw, jnp.concatenate([last, start_grad], axis=0),
        [dtproj_grad, xproj_grad, decay_log_grad, misc],
    )
    if states.ndim == 3:
        states = states.transpose(1, 0, 2).reshape(2 * N, inner)
    input_grad = (
        cotangent[0].astype(F32)
        + inv_rms * gained
        - x * inv_rms * inv_rms * inv_rms * jnp.mean(gained * x, axis=-1, keepdims=True)
    ).astype(BF16)[None]
    if dwo.ndim == 3:
        dwo, dwo_gate = (
            half.reshape(S, R, B, C).transpose(1, 2, 0, 3).reshape(R, S * inner)
            for half in (dwo, dwo_gate)
        )
    raw = jnp.concatenate([dwo, dwo_gate], axis=1).astype(F32)
    in_weight_grad = raw * gain
    gain_grad = jnp.sum(raw * weight_rows, axis=1)
    conv_g, conv_b_g, dt_b_g, skip_g = misc[:taps], misc[taps], misc[taps + 1], misc[taps + 2]
    return (
        block_output, input_grad, states[:N][None], states[N:][None], gain_grad, in_weight_grad,
        conv_g, conv_b_g, xproj_g.T, dtproj_g, dt_b_g, decay_g, skip_g, out_weight_grad,
    )


def solution(mesh):
    both = ("batch", "seq")
    in_specs = (
        P("batch", "seq", None), P("batch", "seq", None), P("batch", None, None), P("batch", None),
        P(both), P(both, None), P(None, both), P(both), P(both, None), P(None, both), P(both),
        P(None, both), P(both), P(both, None),
    )
    out_specs = (
        P("batch", "seq", None), P("batch", "seq", None), P("batch", None, "seq"),
        P("batch", None, "seq"), P(both), P(both, None), P(None, both), P(both), P(both, None),
        P(None, both), P(both), P(None, both), P(both), P(both, None),
    )
    return jax.shard_map(
        functools.partial(body, mesh.shape["batch"], mesh.shape["seq"]),
        mesh=mesh, in_specs=in_specs, out_specs=out_specs, check_vma=False,
    )
```
